32 devices in a mesh: seq: 16 (over z, y, core), rows: 2 (over x).
Axes of the slice: x: 2, y: 2, z: 4, core: 2. Of those that a mesh axis runs over, the one named last changes fastest.
Arguments:
- tokens: bfloat16 [32, 16, 64, 1152], P('seq', 'rows'), may hold values from -6 to 6
- image_ids: int32 [32, 64], P('seq'), may hold values from 0 to 3, as said below
- timestep: int32 [32, 4], P('seq'), may hold values from 0 to 999
- norm1_gain: float32 [1152], replicated, may hold values from 0.1 to 1.9
- norm1_shift: float32 [1152], replicated, may hold values from -3 to 3
- time_in_weight: bfloat16 [256, 1152], P('seq'), may hold values from -0.375 to 0.375
- time_in_bias: float32 [1152], replicated, may hold values from -3 to 3
- time_out_weight: bfloat16 [1152, 1152], P('seq'), may hold values from -0.1875 to 0.1875
- time_out_bias: float32 [1152], replicated, may hold values from -3 to 3
- mix_weight: bfloat16 [1152, 3456], P('seq'), may hold values from -0.1875 to 0.1875
- time_mix_weight: bfloat16 [1152, 3456], P('seq'), may hold values from -0.1875 to 0.1875
- position_bias: float32 [16, 9, 9], replicated, may hold values from -4 to 4
- proj_weight: bfloat16 [1152, 1152], P('seq'), may hold values from -0.5 to 0.5
- proj_bias: float32 [1152], replicated, may hold values from -2 to 2
- norm2_gain: float32 [1152], replicated, may hold values from 0.1 to 1.9
- norm2_shift: float32 [1152], replicated, may hold values from -3 to 3
- up_weight: bfloat16 [1152, 4608], P('seq'), may hold values from -0.1875 to 0.1875
- up_bias: float32 [4608], replicated, may hold values from -3 to 3
- down_weight: bfloat16 [4608, 1152], P('seq'), may hold values from -0.09375 to 0.09375
- down_bias: float32 [1152], replicated, may hold values from -2 to 2
- cotangent: bfloat16 [32, 16, 64, 1152], P('seq', 'rows'), may hold values from -6 to 6
Outputs:
- output: bfloat16 [32, 16, 64, 1152], P('seq', 'rows')
- tokens_grad: bfloat16 [32, 16, 64, 1152], P('seq', 'rows')
- norm1_gain_grad: float32 [1152], replicated
- norm1_shift_grad: float32 [1152], replicated
- time_in_weight_grad: float32 [256, 1152], P('seq')
- time_in_bias_grad: float32 [1152], replicated
- time_out_weight_grad: float32 [1152, 1152], P('seq')
- time_out_bias_grad: float32 [1152], replicated
- mix_weight_grad: float32 [1152, 3456], P('seq')
- time_mix_weight_grad: float32 [1152, 3456], P('seq')
- position_bias_grad: float32 [16, 9, 9], replicated
- proj_weight_grad: float32 [1152, 1152], P('seq')
- proj_bias_grad: float32 [1152], replicated
- norm2_gain_grad: float32 [1152], replicated
- norm2_shift_grad: float32 [1152], replicated
- up_weight_grad: float32 [1152, 4608], P('seq')
- up_bias_grad: float32 [4608], replicated
- down_weight_grad: float32 [4608, 1152], P('seq')
- down_bias_grad: float32 [1152], replicated
The draws below stay inside these ranges and needn't reach their ends.
Inputs may be any that keep to these rules, and one draw needn't show every extreme that they name: `image_ids`: canvas columns k * 16 to (k + 1) * 16 - 1 of a sequence row share one id, and the 4 blocks of a row hold each id once.
All inputs are finite; a program needn't handle non-finite values.
Results may differ from the reference program's by a relative error of at most 0.019.
Values may be sent and summed in bfloat16 or wider, within the bound.
No kernel may reach another device: no remote copies, remote signals or barrier semaphores. Data moves between devices by JAX's collectives and lax.ppermute only.
A program may use at most 640 MiB of HBM per device.

```python
import math
import jax
import jax.numpy as jnp
from jax import lax

D = 1152
HEADS = 16
HEAD_DIM = 72
FF = 4608
FREQ = 256
GRID = 16
PACK = 4
REACH = 4
STEPS = 1000
SEQS = 32


def draw_image_ids(key, part):
    row_keys = jax.random.split(key, SEQS)

    def one_order(row_key):
        return jax.random.permutation(row_key, PACK)
    orders = jax.vmap(one_order)(row_keys)
    return jnp.repeat(orders, GRID, axis=1).astype(jnp.int32)


def set_ends(result, key, least, high):
    shape = result.shape
    spot = [jax.random.randint(jax.random.fold_in(key, axis), (), 0, shape[axis]) for axis in range(len(shape))]
    result = result.at[tuple(spot)].set(least)
    longest = shape.index(max(shape))
    spot[longest] = (spot[longest] + 1) % shape[longest]
    return result.at[tuple(spot)].set(high)


def with_spikes(array, own_key, source, target, blocks, factor):
    owner, partner = [(jnp.arange(array.shape[dim]) // (array.shape[dim] // blocks)).reshape([-1 if axis == dim else 1 for axis in range(array.ndim)]) for dim in (source, target)]
    chosen = jax.random.permutation(own_key, blocks)[partner]
    strong = (owner == chosen) | (owner == (partner + blocks // 2) % blocks)
    return jnp.where(strong, factor * array, array)


def shard_levels(stream_key, shape, shards, smallest, largest):
    def one(axis_at, blocks):
        steps = jax.random.uniform(jax.random.fold_in(jax.random.fold_in(stream_key, 6), axis_at), (blocks,), jnp.float32, smallest / len(shards), largest / len(shards))
        return jnp.repeat(jnp.exp(steps), shape[axis_at] // blocks).reshape((-1,) + (1,) * (len(shape) - axis_at - 1))

    loudness = one(*shards[0])
    for cut in shards[1:]:
        loudness = loudness * one(*cut)
    return loudness


def bell_draw(rng, dims, width, bound, cuts=(), held_as=jnp.bfloat16):
    factor_of = shard_levels(rng, dims, cuts, -0.22, 0.18) if cuts else 1.0
    values = jax.random.normal(rng, dims, jnp.float32) * width * factor_of
    return jnp.minimum(jnp.maximum(values, -bound), bound).astype(held_as)


def gaussian_with(key, extent, width, most, cuts, heavy, kind=jnp.bfloat16):
    array = width * jax.random.normal(key, extent, jnp.float32)
    if cuts:
        array = array * shard_levels(key, extent, cuts, -0.22, 0.18)
    return jnp.clip(with_spikes(array, jax.random.fold_in(key, 3), *heavy), -most, most).astype(kind)


def setup_inputs(seed: int = 0) -> dict:
    key_of = jax.random.split(jax.random.key(seed), 22)
    tokens = gaussian_with(key_of[0], (SEQS, GRID, GRID * PACK, D), 1.0, 6.0, ((0, 16), (1, 2)), (0, 3, 16, 2.0))
    image_ids = draw_image_ids(jax.random.fold_in(key_of[21], 71), 0)
    timestep = set_ends(jax.random.randint(key_of[2], (SEQS, PACK), 0, STEPS), jax.random.fold_in(key_of[2], 1), 0, STEPS - 1).astype(jnp.int32)
    norm1_gain = jnp.clip(1.0 + 0.18 * jax.random.normal(key_of[3], (D,), jnp.float32), 0.1, 1.9)
    norm1_shift = bell_draw(key_of[4], (D,), 0.5, 3.0, (), jnp.float32)
    time_in_weight = bell_draw(key_of[5], (FREQ, D), FREQ ** -0.5, 0.375, ((0, 16),))
    time_in_bias = bell_draw(key_of[6], (D,), 0.5, 3.0, (), jnp.float32)
    time_out_weight = bell_draw(key_of[7], (D, D), D ** -0.5, 0.1875, ((0, 16),))
    time_out_bias = bell_draw(key_of[8], (D,), 0.5, 3.0, (), jnp.float32)
    mix_weight = bell_draw(key_of[9], (D, 3 * D), D ** -0.5, 0.1875, ((0, 16),))
    time_mix_weight = bell_draw(key_of[10], (D, 3 * D), D ** -0.5, 0.1875, ((0, 16),))
    position_bias = bell_draw(key_of[11], (HEADS, 2 * REACH + 1, 2 * REACH + 1), 1.0, 4.0, (), jnp.float32)
    proj_weight = bell_draw(key_of[12], (D, D), (D // 9) ** -0.5, 0.5, ((0, 16),))
    proj_bias = bell_draw(key_of[13], (D,), 0.3, 2.0, (), jnp.float32)
    norm2_gain = jnp.clip(1.0 + 0.18 * jax.random.normal(key_of[14], (D,), jnp.float32), 0.1, 1.9)
    norm2_shift = bell_draw(key_of[15], (D,), 0.5, 3.0, (), jnp.float32)
    up_weight = bell_draw(key_of[16], (D, FF), D ** -0.5, 0.1875, ((0, 16),))
    up_bias = bell_draw(key_of[17], (FF,), 0.5, 3.0, (), jnp.float32)
    down_weight = bell_draw(key_of[18], (FF, D), FF ** -0.5, 0.09375, ((0, 16),))
    down_bias = bell_draw(key_of[19], (D,), 0.3, 2.0, (), jnp.float32)
    cotangent = gaussian_with(key_of[20], (SEQS, GRID, GRID * PACK, D), 1.0, 6.0, ((0, 16), (1, 2)), (0, 3, 16, 2.0))
    return {"tokens": tokens, "image_ids": image_ids, "timestep": timestep, "norm1_gain": norm1_gain, "norm1_shift": norm1_shift, "time_in_weight": time_in_weight, "time_in_bias": time_in_bias, "time_out_weight": time_out_weight, "time_out_bias": time_out_bias, "mix_weight": mix_weight, "time_mix_weight": time_mix_weight, "position_bias": position_bias, "proj_weight": proj_weight, "proj_bias": proj_bias, "norm2_gain": norm2_gain, "norm2_shift": norm2_shift, "up_weight": up_weight, "up_bias": up_bias, "down_weight": down_weight, "down_bias": down_bias, "cotangent": cotangent}


@jax.custom_vjp
def low(v):
    return lax.optimization_barrier(v.astype(jnp.bfloat16)).astype(jnp.float32)

@jax.custom_vjp
def low_back(v):
    return v

def low_keep(v):
    return (low(v), None)

def low_pass(kept, grad):
    return (grad,)

def back_keep(v):
    return (v, None)

def back_low(kept, grad):
    return (low(grad),)
low.defvjp(low_keep, low_pass)
low_back.defvjp(back_keep, back_low)
epsilon = 1e-06
floor_score = -1e+30
highest = lax.Precision.HIGHEST

def full_dot(left, right):
    return jnp.dot(left, right, precision=highest, preferred_element_type=jnp.float32)

def layer_norm(values, norm_gain, norm_shift):
    centred = values - lax.optimization_barrier(jnp.mean(values, axis=-1, keepdims=True))
    variance = lax.optimization_barrier(jnp.mean(centred * centred, axis=-1, keepdims=True))
    return centred * lax.rsqrt(variance + epsilon) * norm_gain + norm_shift

def forward(tokens, image_ids, timestep, norm1_gain, norm1_shift, time_in_weight, time_in_bias, time_out_weight, time_out_bias, mix_weight, time_mix_weight, position_bias, proj_weight, proj_bias, norm2_gain, norm2_shift, up_weight, up_bias, down_weight, down_bias):
    seq_count = tokens.shape[0]
    columns = GRID * PACK
    length = GRID * columns
    half_width = FREQ // 2
    frequency = jnp.exp(-math.log(10000.0) * jnp.arange(half_width, dtype=jnp.float32) / half_width)
    angles = timestep.astype(jnp.float32)[:, :, None] * frequency
    features = low(jnp.concatenate([jnp.cos(angles), jnp.sin(angles)], axis=-1))
    time_pre = full_dot(features, time_in_weight) + time_in_bias
    time_hidden = low(jax.nn.silu(time_pre))
    time_embed = low(full_dot(time_hidden, time_out_weight) + time_out_bias)
    time_proj = full_dot(time_embed, time_mix_weight)
    flat_tokens = tokens.reshape(seq_count, length, D)
    normed1 = low(layer_norm(flat_tokens, norm1_gain, norm1_shift))
    positions = jnp.arange(length)
    pos_row = positions // columns
    pos_col = positions % columns
    token_ids = image_ids[:, pos_col]
    image_hot = (token_ids[:, :, None] == jnp.arange(PACK, dtype=jnp.int32)[None, None, :]).astype(jnp.float32)
    mixed_proj = full_dot(normed1, mix_weight) + jnp.einsum('slp,spe->sle', image_hot, time_proj, precision=highest)
    queries = low_back(low(mixed_proj[..., :D])).reshape(seq_count, length, HEADS, HEAD_DIM)
    key_rows = low_back(low(mixed_proj[..., D:2 * D])).reshape(seq_count, length, HEADS, HEAD_DIM)
    value_rows = low_back(low(mixed_proj[..., 2 * D:])).reshape(seq_count, length, HEADS, HEAD_DIM)
    row_diff = pos_row[None, :] - pos_row[:, None]
    col_diff = pos_col[None, :] - pos_col[:, None]
    near_mask = (jnp.abs(row_diff) <= REACH) & (jnp.abs(col_diff) <= REACH)
    row_index = jnp.clip(row_diff, -REACH, REACH) + REACH
    col_index = jnp.clip(col_diff, -REACH, REACH) + REACH
    score_scale = HEAD_DIM ** (-0.5)

    def attend(inputs):
        seq_queries, seq_keys, seq_values, seq_ids = inputs
        bias_table = position_bias[:, row_index, col_index]
        allowed = near_mask & (seq_ids[:, None] == seq_ids[None, :])
        scores = jnp.einsum('qhd,khd->hqk', seq_queries, seq_keys, precision=highest) * score_scale + bias_table
        scores = jnp.where(allowed[None], low_back(scores), floor_score)
        row_top = lax.optimization_barrier(jnp.max(scores, axis=-1, keepdims=True))
        row_total = lax.optimization_barrier(jnp.sum(jnp.exp(scores - row_top), axis=-1, keepdims=True))
        log_total = row_top + jnp.log(row_total)
        probability = low(jnp.exp(scores - log_total))
        return jnp.einsum('hqk,khd->qhd', probability, seq_values, precision=highest)
    attended = lax.map(jax.checkpoint(attend), (queries, key_rows, value_rows, token_ids))
    attended = low_back(low(attended.reshape(seq_count, length, D)))
    branch = low_back(full_dot(attended, proj_weight) + proj_bias)
    residual = flat_tokens + branch
    normed2 = low(layer_norm(residual, norm2_gain, norm2_shift))
    hidden_pre = low_back(full_dot(normed2, up_weight) + up_bias)
    hidden = low(jax.nn.gelu(hidden_pre, approximate=True))
    down_out = low_back(full_dot(hidden, down_weight) + down_bias)
    return (residual + down_out).reshape(tokens.shape)

def reference(tokens, image_ids, timestep, norm1_gain, norm1_shift, time_in_weight, time_in_bias, time_out_weight, time_out_bias, mix_weight, time_mix_weight, position_bias, proj_weight, proj_bias, norm2_gain, norm2_shift, up_weight, up_bias, down_weight, down_bias, cotangent):
    floats = (tokens, norm1_gain, norm1_shift, time_in_weight, time_in_bias, time_out_weight, time_out_bias, mix_weight, time_mix_weight, position_bias, proj_weight, proj_bias, norm2_gain, norm2_shift, up_weight, up_bias, down_weight, down_bias)
    floats = tuple((array_value.astype(jnp.float32) for array_value in floats))

    def apply_layer(*values):
        return forward(values[0], image_ids, timestep, *values[1:])
    output, pullback = jax.vjp(apply_layer, *floats)
    gradients = pullback(cotangent.astype(jnp.float32))
    return (output.astype(jnp.bfloat16), gradients[0].astype(jnp.bfloat16), gradients[1], gradients[2], gradients[3], gradients[4], gradients[5], gradients[6], gradients[7], gradients[8], gradients[9], gradients[10], gradients[11], gradients[12], gradients[13], gradients[14], gradients[15], gradients[16], gradients[17])
```

```python
import functools
import math

import jax
import jax.numpy as jnp
from jax import lax
from jax.experimental import pallas as pl
from jax.experimental.pallas import tpu as pltpu
from jax.sharding import PartitionSpec as P

D = 1152
HEADS = 16
HEAD_DIM = 72
FF = 4608
FREQ = 256
GRID = 16
PACK = 4
REACH = 4
LANES = 128


epsilon = 1e-06
floor_score = -1e30
highest = lax.Precision.HIGHEST
score_scale = HEAD_DIM ** (-0.5)


def low_dot(left, right):
    return jnp.dot(left, right, preferred_element_type=jnp.float32)


def gelu_tanh(values):
    return jax.nn.gelu(values, approximate=True)


def norm_forward(values, norm_gain, norm_shift):
    centred = values - jnp.mean(values, axis=-1, keepdims=True)
    inverse = lax.rsqrt(jnp.mean(centred * centred, axis=-1, keepdims=True) + epsilon)
    unit_rows = centred * inverse
    return (unit_rows * norm_gain + norm_shift, unit_rows, inverse)


def norm_backward(grad_out, unit_rows, inverse, norm_gain):
    scaled = grad_out * norm_gain
    grad_in = inverse * (
        scaled
        - jnp.mean(scaled, axis=-1, keepdims=True)
        - unit_rows * jnp.mean(scaled * unit_rows, axis=-1, keepdims=True)
    )
    leading = tuple(range(grad_out.ndim - 1))
    return (grad_in, jnp.sum(grad_out * unit_rows, axis=leading), jnp.sum(grad_out, axis=leading))


def row_plan(local_rows, shards):
    if shards == 2 and local_rows >= REACH:
        return (True, 1, REACH)
    sent = min(local_rows, REACH)
    return (False, -(-REACH // local_rows), sent)


def route(shards, distance):
    return [(i - distance, i) for i in range(shards) if 0 <= i - distance < shards]


def borrow_rows(own, shards):
    rows = own.shape[1]
    one_sided, turns, sent = row_plan(rows, shards)
    place = lax.axis_index("rows")
    if one_sided:
        start = jnp.where(place == 0, rows - sent, 0)
        block = lax.dynamic_slice_in_dim(own, start, sent, axis=1)
        got = lax.ppermute(block, "rows", [(0, 1), (1, 0)])
        first = jnp.where(place == 0, rows, -sent)
        return (got, first + jnp.arange(sent))
    pieces, where = [], []
    for turn in range(turns, 0, -1):
        pieces.append(lax.ppermute(own[:, rows - sent :], "rows", route(shards, turn)))
        where.append(jnp.arange(sent) - (turn - 1) * rows - sent)
    for turn in range(1, turns + 1):
        pieces.append(lax.ppermute(own[:, :sent], "rows", route(shards, -turn)))
        where.append(jnp.arange(sent) + turn * rows)
    return (jnp.concatenate(pieces, axis=1), jnp.concatenate(where))


def return_rows(own, borrowed, shards):
    rows = own.shape[1]
    one_sided, turns, sent = row_plan(rows, shards)
    place = lax.axis_index("rows")
    borrowed = borrowed.astype(jnp.bfloat16)
    if one_sided:
        got = lax.ppermute(borrowed, "rows", [(0, 1), (1, 0)]).astype(own.dtype)
        room = [(0, 0)] * own.ndim
        at_end, at_start = list(room), list(room)
        at_end[1], at_start[1] = (rows - sent, 0), (0, rows - sent)
        return own + jnp.where(place == 0, jnp.pad(got, at_end), jnp.pad(got, at_start))
    piece = 0
    for turn in range(turns, 0, -1):
        back = lax.ppermute(borrowed[:, piece * sent : (piece + 1) * sent], "rows", route(shards, -turn))
        own = own.at[:, rows - sent :].add(back.astype(own.dtype))
        piece += 1
    for turn in range(1, turns + 1):
        back = lax.ppermute(borrowed[:, piece * sent : (piece + 1) * sent], "rows", route(shards, turn))
        own = own.at[:, :sent].add(back.astype(own.dtype))
        piece += 1
    return own


def head_window(head):
    first, last = head * HEAD_DIM, (head + 1) * HEAD_DIM
    return (first // LANES * LANES, -(-last // LANES) * LANES)


def head_mask(head, dtype):
    low, high = head_window(head)
    lane = lax.broadcasted_iota(jnp.int32, (1, high - low), 1) + low
    return ((lane >= head * HEAD_DIM) & (lane < (head + 1) * HEAD_DIM)).astype(dtype)


def nt_dot(left, right):
    return lax.dot_general(left, right, (((1,), (1,)), ((), ())), preferred_element_type=jnp.float32)


def tn_dot(left, right):
    return lax.dot_general(left, right, (((0,), (0,)), ((), ())), preferred_element_type=jnp.float32)


def attend_kernel(mixed_ref, table_ref, out_ref, acc_ref, *, own, total):
    def columns(part, low, high, count):
        block = mixed_ref[0, : count // GRID, 0, :, part * D + low : part * D + high]
        return block.reshape(count, high - low)

    for head in range(HEADS):
        low, high = head_window(head)
        keep = head_mask(head, jnp.bfloat16)
        query = columns(0, low, high, own) * keep
        scores = nt_dot(query, columns(1, low, high, total)) * score_scale + table_ref[head]
        top = jnp.max(scores, axis=1, keepdims=True)
        weight = jnp.exp(scores - top)
        weight = weight * (1.0 / jnp.sum(weight, axis=1, keepdims=True))
        result = low_dot(weight.astype(jnp.bfloat16), columns(2, low, high, total))
        mine = head_mask(head, jnp.float32)
        if head == 0:
            acc_ref[:, low:high] = result
        else:
            earlier = acc_ref[:, low : low + LANES]
            acc_ref[:, low : low + LANES] = jnp.where(mine[:, :LANES] > 0, result[:, :LANES], earlier)
            if high - low > LANES:
                acc_ref[:, low + LANES : high] = result[:, LANES:]
    out_ref[0, :, 0] = acc_ref[...].astype(jnp.bfloat16).reshape(own // GRID, GRID, D)


def attend_back_kernel(mixed_ref, grad_ref, table_ref, out_ref, bias_ref, q_ref, k_ref, v_ref, *, own, total):
    @pl.when((pl.program_id(0) == 0) & (pl.program_id(1) == 0))
    def _():
        bias_ref[...] = jnp.zeros_like(bias_ref)

    def columns(part, low, high, count):
        block = mixed_ref[0, : count // GRID, 0, :, part * D + low : part * D + high]
        return block.reshape(count, high - low)

    def put(ref, low, high, value, fresh):
        if fresh:
            ref[:, low:high] = value
        else:
            ref[:, low : low + LANES] += value[:, :LANES]
            if high - low > LANES:
                ref[:, low + LANES : high] = value[:, LANES:]

    for head in range(HEADS):
        low, high = head_window(head)
        fresh = head * HEAD_DIM % LANES == 0
        keep = head_mask(head, jnp.bfloat16)
        query = columns(0, low, high, own) * keep
        grad = grad_ref[0, :, 0, :, low:high].reshape(own, high - low) * keep
        keys = columns(1, low, high, total)
        scores = nt_dot(keys, query) * score_scale + table_ref[head]
        top = jnp.max(scores, axis=0, keepdims=True)
        weight = jnp.exp(scores - top)
        weight = weight * (1.0 / jnp.sum(weight, axis=0, keepdims=True))
        grad_weight = nt_dot(columns(2, low, high, total), grad)
        delta = jnp.sum(weight * grad_weight, axis=0, keepdims=True)
        grad_scores = weight * (grad_weight - delta)
        bias_ref[head] += grad_scores
        grad_low = grad_scores.astype(jnp.bfloat16)
        put(v_ref, low, high, low_dot(weight.astype(jnp.bfloat16), grad), fresh)
        put(k_ref, low, high, low_dot(grad_low, query), fresh)
        put(q_ref, low, high, tn_dot(grad_low, keys) * head_mask(head, jnp.float32), fresh)
    rows, own_rows = total // GRID, own // GRID
    out_ref[0, :own_rows, 0, :, :D] = (q_ref[...] * score_scale).astype(jnp.bfloat16).reshape(own_rows, GRID, D)
    if rows > own_rows:
        out_ref[0, own_rows:, 0, :, :D] = jnp.zeros((rows - own_rows, GRID, D), jnp.bfloat16)
    out_ref[0, :, 0, :, D : 2 * D] = (k_ref[...] * score_scale).astype(jnp.bfloat16).reshape(rows, GRID, D)
    out_ref[0, :, 0, :, 2 * D :] = v_ref[...].astype(jnp.bfloat16).reshape(rows, GRID, D)


def attend(mixed, table, own_rows):
    seqs, rows = mixed.shape[:2]
    own, total = own_rows * GRID, rows * GRID
    return pl.pallas_call(
        functools.partial(attend_kernel, own=own, total=total),
        grid=(seqs, PACK),
        in_specs=[
            pl.BlockSpec((1, rows, 1, GRID, 3 * D), lambda s, p: (s, 0, p, 0, 0)),
            pl.BlockSpec((HEADS, own, total), lambda s, p: (0, 0, 0)),
        ],
        out_specs=pl.BlockSpec((1, own_rows, 1, GRID, D), lambda s, p: (s, 0, p, 0, 0)),
        out_shape=jax.ShapeDtypeStruct((seqs, own_rows, PACK, GRID, D), jnp.bfloat16),
        scratch_shapes=[pltpu.VMEM((own, D), jnp.float32)],
        compiler_params=pltpu.CompilerParams(
            dimension_semantics=("arbitrary", "arbitrary"), vmem_limit_bytes=48 << 20
        ),
        name="attend",
    )(mixed, table)


def attend_back(mixed, grad, table, own_rows):
    seqs, rows = mixed.shape[:2]
    own, total = own_rows * GRID, rows * GRID
    return pl.pallas_call(
        functools.partial(attend_back_kernel, own=own, total=total),
        grid=(seqs, PACK),
        in_specs=[
            pl.BlockSpec((1, rows, 1, GRID, 3 * D), lambda s, p: (s, 0, p, 0, 0)),
            pl.BlockSpec((1, own_rows, 1, GRID, D), lambda s, p: (s, 0, p, 0, 0)),
            pl.BlockSpec((HEADS, total, own), lambda s, p: (0, 0, 0)),
        ],
        out_specs=[
            pl.BlockSpec((1, rows, 1, GRID, 3 * D), lambda s, p: (s, 0, p, 0, 0)),
            pl.BlockSpec((HEADS, total, own), lambda s, p: (0, 0, 0)),
        ],
        out_shape=[
            jax.ShapeDtypeStruct((seqs, rows, PACK, GRID, 3 * D), jnp.bfloat16),
            jax.ShapeDtypeStruct((HEADS, total, own), jnp.float32),
        ],
        scratch_shapes=[
            pltpu.VMEM((own, D), jnp.float32),
            pltpu.VMEM((total, D), jnp.float32),
            pltpu.VMEM((total, D), jnp.float32),
        ],
        compiler_params=pltpu.CompilerParams(
            dimension_semantics=("arbitrary", "arbitrary"), vmem_limit_bytes=48 << 20
        ),
        name="attend_back",
    )(mixed, grad, table)


def on_device(
    row_shards,
    tokens,
    image_ids,
    timestep,
    norm1_gain,
    norm1_shift,
    time_in_weight,
    time_in_bias,
    time_out_weight,
    time_out_bias,
    mix_weight,
    time_mix_weight,
    position_bias,
    proj_weight,
    proj_bias,
    norm2_gain,
    norm2_shift,
    up_weight,
    up_bias,
    down_weight,
    down_bias,
    cotangent,
):
    seq_rows, local_rows, columns, _ = tokens.shape
    act_tokens = tokens.reshape(seq_rows, local_rows, PACK, GRID, D)
    act_cot = cotangent.reshape(seq_rows, local_rows, PACK, GRID, D)
    token_count = seq_rows * local_rows * columns
    borrowed, borrowed_at = borrow_rows(act_tokens, row_shards)
    ext_tokens = jnp.concatenate([act_tokens, borrowed], axis=1)
    ext_rows = ext_tokens.shape[1]
    ext_count = seq_rows * ext_rows * columns
    full_mix, full_tin, full_tout, full_tmix, full_proj, full_up, full_down = (
        lax.all_gather(mix_weight, "seq", axis=0, tiled=True),
        lax.all_gather(time_in_weight, "seq", axis=0, tiled=True),
        lax.all_gather(time_out_weight, "seq", axis=0, tiled=True),
        lax.all_gather(time_mix_weight, "seq", axis=0, tiled=True),
        lax.all_gather(proj_weight, "seq", axis=0, tiled=True),
        lax.all_gather(up_weight, "seq", axis=0, tiled=True),
        lax.all_gather(down_weight, "seq", axis=0, tiled=True),
    )

    key_at = jnp.concatenate([jnp.arange(local_rows), borrowed_at])
    row_diff = key_at[None, :] - jnp.arange(local_rows)[:, None]
    key_row = lax.axis_index("rows") * local_rows + key_at
    row_valid = (key_row >= 0) & (key_row < GRID)
    col_diff = jnp.arange(GRID)[None, :] - jnp.arange(GRID)[:, None]
    offsets = jnp.arange(2 * REACH + 1) - REACH
    row_hot = (row_diff[:, :, None] == offsets[None, None, :]).astype(jnp.float32)
    col_hot = (col_diff[:, :, None] == offsets[None, None, :]).astype(jnp.float32)
    allowed = (
        (jnp.abs(row_diff) <= REACH)[:, None, :, None]
        & row_valid[None, None, :, None]
        & (jnp.abs(col_diff) <= REACH)[None, :, None, :]
    )
    own, total = local_rows * GRID, ext_rows * GRID
    table = jnp.einsum("hno,abn,ceo->hacbe", position_bias, row_hot, col_hot, precision=highest)
    table = jnp.where(allowed, table, floor_score).reshape(HEADS, own, total)
    table_back = jnp.swapaxes(table, 1, 2)

    half_width = FREQ // 2
    frequency = jnp.exp(-math.log(10000.0) * jnp.arange(half_width, dtype=jnp.float32) / half_width)
    angles = timestep.astype(jnp.float32)[:, :, None] * frequency
    features = jnp.concatenate([jnp.cos(angles), jnp.sin(angles)], axis=-1).astype(jnp.bfloat16)
    time_pre = low_dot(features, full_tin) + time_in_bias
    time_hidden = jax.nn.silu(time_pre).astype(jnp.bfloat16)
    time_embed = (low_dot(time_hidden, full_tout) + time_out_bias).astype(jnp.bfloat16)
    time_proj = low_dot(time_embed, full_tmix)
    block_slots = image_ids[:, ::GRID]
    slot_hot = (block_slots[:, :, None] == jnp.arange(PACK, dtype=jnp.int32)[None, None, :]).astype(
        jnp.float32
    )
    unit_total = seq_rows * PACK
    unit_time = jnp.einsum("skp,spe->ske", slot_hot, time_proj, precision=highest)

    ext_float = ext_tokens.astype(jnp.float32)
    normed1, unit_one, inverse_one = norm_forward(ext_float, norm1_gain, norm1_shift)
    normed1 = normed1.astype(jnp.bfloat16)
    unit_one, inverse_one = unit_one[:, :local_rows], inverse_one[:, :local_rows]
    mixed = (low_dot(normed1, full_mix) + unit_time[:, None, :, None, :]).astype(jnp.bfloat16)
    attended = attend(mixed, table, local_rows)

    flat_tokens = act_tokens.astype(jnp.float32)
    branch = low_dot(attended, full_proj) + proj_bias
    residual = flat_tokens + branch
    normed2, unit_two, inverse_two = norm_forward(residual, norm2_gain, norm2_shift)
    normed2 = normed2.astype(jnp.bfloat16)
    hidden_pre = low_dot(normed2, full_up) + up_bias
    hidden = gelu_tanh(hidden_pre).astype(jnp.bfloat16)
    output = (residual + low_dot(hidden, full_down) + down_bias).astype(jnp.bfloat16)
    flat_hidden = hidden.reshape(token_count, FF)
    flat_cot = act_cot.reshape(token_count, D)
    grad_down_w = jnp.einsum("nf,nd->fd", flat_hidden, flat_cot, preferred_element_type=jnp.float32)
    grad_down_b = jnp.sum(flat_cot, axis=0, dtype=jnp.float32)
    grad_hidden = jnp.einsum("nd,fd->nf", flat_cot, full_down, preferred_element_type=jnp.float32)
    gelu_back = jax.vjp(gelu_tanh, hidden_pre.reshape(token_count, FF))[1]
    grad_pre = gelu_back(grad_hidden)[0].astype(jnp.bfloat16)
    flat_normed2 = normed2.reshape(token_count, D)
    grad_up_w = jnp.einsum("nd,nf->df", flat_normed2, grad_pre, preferred_element_type=jnp.float32)
    grad_up_b = jnp.sum(grad_pre, axis=0, dtype=jnp.float32)
    grad_normed2 = jnp.einsum(
        "nf,df->nd", grad_pre, full_up, preferred_element_type=jnp.float32
    ).reshape(act_tokens.shape)
    grad_norm_two, grad_gain_two, grad_shift_two = norm_backward(
        grad_normed2, unit_two, inverse_two, norm2_gain
    )
    grad_residual = act_cot.astype(jnp.float32) + grad_norm_two
    grad_branch = grad_residual.astype(jnp.bfloat16).reshape(token_count, D)
    grad_proj_w = jnp.einsum(
        "nd,ne->de",
        attended.reshape(token_count, D),
        grad_branch,
        preferred_element_type=jnp.float32,
    )
    grad_proj_b = jnp.sum(grad_branch, axis=0, dtype=jnp.float32)
    grad_attended = jnp.einsum(
        "ne,de->nd", grad_branch, full_proj, preferred_element_type=jnp.float32
    ).astype(jnp.bfloat16)

    grad_mixed, grad_table = attend_back(
        mixed, grad_attended.reshape(act_tokens.shape), table_back, local_rows
    )
    grad_table = grad_table.reshape(HEADS, ext_rows, GRID, local_rows, GRID)
    col_summed = jnp.einsum("hbeac,ceo->hbao", grad_table, col_hot, precision=highest)
    bias_grad = jnp.einsum("hbao,abn->hno", col_summed, row_hot, precision=highest)

    flat_mixed = grad_mixed.reshape(ext_count, 3 * D)
    grad_mix_w = jnp.einsum(
        "nd,ne->de", normed1.reshape(ext_count, D), flat_mixed, preferred_element_type=jnp.float32
    )
    grad_normed1 = jnp.einsum(
        "ne,de->nd", flat_mixed, full_mix, preferred_element_type=jnp.float32
    ).reshape(ext_tokens.shape)
    grad_normed1 = return_rows(
        grad_normed1[:, :local_rows], grad_normed1[:, local_rows:], row_shards
    )
    grad_unit = jnp.sum(grad_mixed, axis=(1, 3), dtype=jnp.float32)
    grad_time_proj = jnp.einsum("skp,ske->spe", slot_hot, grad_unit, precision=highest)
    grad_tmix_w = jnp.einsum(
        "spd,spe->de", time_embed.astype(jnp.float32), grad_time_proj, precision=highest
    )
    grad_embed = jnp.einsum(
        "spe,de->spd", grad_time_proj, full_tmix.astype(jnp.float32), precision=highest
    )
    grad_tout_w = jnp.einsum(
        "spd,spe->de", time_hidden.astype(jnp.float32), grad_embed, precision=highest
    )
    grad_tout_b = jnp.sum(grad_embed, axis=(0, 1))
    grad_thidden = jnp.einsum(
        "spe,de->spd", grad_embed, full_tout.astype(jnp.float32), precision=highest
    )
    silu_back = jax.vjp(jax.nn.silu, time_pre)[1]
    grad_tpre = silu_back(grad_thidden)[0]
    grad_tin_w = jnp.einsum(
        "spf,spd->fd", features.astype(jnp.float32), grad_tpre, precision=highest
    )
    grad_tin_b = jnp.sum(grad_tpre, axis=(0, 1))
    grad_norm_one, grad_gain_one, grad_shift_one = norm_backward(
        grad_normed1, unit_one, inverse_one, norm1_gain
    )
    tokens_grad = (grad_residual + grad_norm_one).astype(jnp.bfloat16)

    def scattered(grad):
        part = lax.psum_scatter(grad.astype(jnp.bfloat16), "seq", scatter_dimension=0, tiled=True)
        return lax.psum(part, "rows").astype(jnp.float32)

    sum_down, sum_up, sum_proj, sum_tin, sum_tout, sum_tmix, sum_mix = (
        scattered(grad_down_w),
        scattered(grad_up_w),
        scattered(grad_proj_w),
        scattered(grad_tin_w),
        scattered(grad_tout_w),
        scattered(grad_tmix_w),
        scattered(grad_mix_w),
    )
    (
        gain_one,
        shift_one,
        tin_bias,
        tout_bias,
        bias_total,
        proj_total,
        gain_two,
        shift_two,
        up_total,
        down_total,
    ) = lax.psum(
        (
            grad_gain_one,
            grad_shift_one,
            grad_tin_b,
            grad_tout_b,
            bias_grad,
            grad_proj_b,
            grad_gain_two,
            grad_shift_two,
            grad_up_b,
            grad_down_b,
        ),
        ("seq", "rows"),
    )
    output = output.reshape(tokens.shape)
    tokens_grad = tokens_grad.reshape(tokens.shape)
    return (
        output,
        tokens_grad,
        gain_one,
        shift_one,
        sum_tin,
        tin_bias,
        sum_tout,
        tout_bias,
        sum_mix,
        sum_tmix,
        bias_total,
        sum_proj,
        proj_total,
        gain_two,
        shift_two,
        sum_up,
        up_total,
        sum_down,
        down_total,
    )


def solution(mesh):
    whole, sharded = (P(), P("seq", None))
    acts = P("seq", "rows", None, None)
    return jax.shard_map(
        functools.partial(on_device, mesh.shape["rows"]),
        mesh=mesh,
        in_specs=(
            acts,
            sharded,
            sharded,
            whole,
            whole,
            sharded,
            whole,
            sharded,
            whole,
            sharded,
            sharded,
            whole,
            sharded,
            whole,
            whole,
            whole,
            sharded,
            whole,
            sharded,
            whole,
            acts,
        ),
        out_specs=(
            acts,
            acts,
            whole,
            whole,
            sharded,
            whole,
            sharded,
            whole,
            sharded,
            sharded,
            whole,
            sharded,
            whole,
            whole,
            whole,
            sharded,
            whole,
            sharded,
            whole,
        ),
        check_vma=False,
    )
```

```python
import functools
import math

import jax
import jax.numpy as jnp
from jax import lax
from jax.experimental import pallas as pl
from jax.experimental.pallas import tpu as pltpu
from jax.sharding import PartitionSpec as P

D = 1152
HEADS = 16
HEAD_DIM = 72
FF = 4608
FREQ = 256
GRID = 16
PACK = 4
REACH = 4
LANES = 128


epsilon = 1e-06
floor_score = -1e30
highest = lax.Precision.HIGHEST
score_scale = HEAD_DIM ** (-0.5)


def low_dot(left, right):
    return jnp.dot(left, right, preferred_element_type=jnp.float32)


def gelu_tanh(values):
    return jax.nn.gelu(values, approximate=True)


def norm_forward(values, norm_gain, norm_shift):
    centred = values - jnp.mean(values, axis=-1, keepdims=True)
    inverse = lax.rsqrt(jnp.mean(centred * centred, axis=-1, keepdims=True) + epsilon)
    unit_rows = centred * inverse
    return (unit_rows * norm_gain + norm_shift, unit_rows, inverse)


def norm_backward(grad_out, unit_rows, inverse, norm_gain):
    scaled = grad_out * norm_gain
    grad_in = inverse * (
        scaled
        - jnp.mean(scaled, axis=-1, keepdims=True)
        - unit_rows * jnp.mean(scaled * unit_rows, axis=-1, keepdims=True)
    )
    leading = tuple(range(grad_out.ndim - 1))
    return (grad_in, jnp.sum(grad_out * unit_rows, axis=leading), jnp.sum(grad_out, axis=leading))


def row_plan(local_rows, shards):
    if shards == 2 and local_rows >= REACH:
        return (True, 1, REACH)
    sent = min(local_rows, REACH)
    return (False, -(-REACH // local_rows), sent)


def route(shards, distance):
    return [(i - distance, i) for i in range(shards) if 0 <= i - distance < shards]


def borrow_rows(own, shards):
    rows = own.shape[1]
    one_sided, turns, sent = row_plan(rows, shards)
    place = lax.axis_index("rows")
    if one_sided:
        start = jnp.where(place == 0, rows - sent, 0)
        block = lax.dynamic_slice_in_dim(own, start, sent, axis=1)
        got = lax.ppermute(block, "rows", [(0, 1), (1, 0)])
        first = jnp.where(place == 0, rows, -sent)
        return (got, first + jnp.arange(sent), block)
    pieces, where = [], []
    for turn in range(turns, 0, -1):
        pieces.append(lax.ppermute(own[:, rows - sent :], "rows", route(shards, turn)))
        where.append(jnp.arange(sent) - (turn - 1) * rows - sent)
    for turn in range(1, turns + 1):
        pieces.append(lax.ppermute(own[:, :sent], "rows", route(shards, -turn)))
        where.append(jnp.arange(sent) + turn * rows)
    return (jnp.concatenate(pieces, axis=1), jnp.concatenate(where), own[:, :sent])


def return_rows(own, borrowed, shards):
    rows = own.shape[1]
    one_sided, turns, sent = row_plan(rows, shards)
    place = lax.axis_index("rows")
    borrowed = borrowed.astype(jnp.bfloat16)
    if one_sided:
        got = lax.ppermute(borrowed, "rows", [(0, 1), (1, 0)]).astype(own.dtype)
        room = [(0, 0)] * own.ndim
        at_end, at_start = list(room), list(room)
        at_end[1], at_start[1] = (rows - sent, 0), (0, rows - sent)
        return own + jnp.where(place == 0, jnp.pad(got, at_end), jnp.pad(got, at_start))
    piece = 0
    for turn in range(turns, 0, -1):
        back = lax.ppermute(borrowed[:, piece * sent : (piece + 1) * sent], "rows", route(shards, -turn))
        own = own.at[:, rows - sent :].add(back.astype(own.dtype))
        piece += 1
    for turn in range(1, turns + 1):
        back = lax.ppermute(borrowed[:, piece * sent : (piece + 1) * sent], "rows", route(shards, turn))
        own = own.at[:, :sent].add(back.astype(own.dtype))
        piece += 1
    return own


def head_window(head):
    first, last = head * HEAD_DIM, (head + 1) * HEAD_DIM
    return (first // LANES * LANES, -(-last // LANES) * LANES)


def head_mask(head, dtype):
    low, high = head_window(head)
    lane = lax.broadcasted_iota(jnp.int32, (1, high - low), 1) + low
    return ((lane >= head * HEAD_DIM) & (lane < (head + 1) * HEAD_DIM)).astype(dtype)


def nt_dot(left, right):
    return lax.dot_general(left, right, (((1,), (1,)), ((), ())), preferred_element_type=jnp.float32)


def tn_dot(left, right):
    return lax.dot_general(left, right, (((0,), (0,)), ((), ())), preferred_element_type=jnp.float32)


def table_kernel(bias_ref, row_ref, out_ref, *, own, rows):
    head = pl.program_id(0)
    reach = 2 * REACH + 1
    lane = lax.broadcasted_iota(jnp.int32, (GRID, own), 1)
    query_row, query_col = lane // GRID, lane % GRID
    col_diff = lax.broadcasted_iota(jnp.int32, (GRID, own), 0) - query_col
    floor = jnp.full((GRID, own), floor_score, jnp.float32)
    by_row = []
    for n in range(reach):
        value = floor
        for o in range(reach):
            value = jnp.where(col_diff == o - REACH, bias_ref[head, n * reach + o], value)
        by_row.append(value)
    for b in range(rows):
        row_diff = row_ref[b] - query_row
        value = floor
        for n in range(reach):
            value = jnp.where(row_diff == n - REACH, by_row[n], value)
        out_ref[0, b * GRID : (b + 1) * GRID, :] = value


def bias_table(position_bias, key_rows, own_rows):
    rows = key_rows.shape[0]
    own, total = own_rows * GRID, rows * GRID
    smem = pl.BlockSpec(memory_space=pltpu.SMEM)
    return pl.pallas_call(
        functools.partial(table_kernel, own=own, rows=rows),
        grid=(HEADS,),
        in_specs=[smem, smem],
        out_specs=pl.BlockSpec((1, total, own), lambda h: (h, 0, 0)),
        out_shape=jax.ShapeDtypeStruct((HEADS, total, own), jnp.float32),
        name="bias_table",
    )(position_bias.reshape(HEADS, -1), key_rows)


def assemble_kernel(at_ref, *refs):
    pieces, out_ref, room, into, out_of = refs[:-4], refs[-4], refs[-3], refs[-2], refs[-1]
    first = [pltpu.make_async_copy(piece, room.at[i], into.at[i]) for i, piece in enumerate(pieces)]
    second = [pltpu.make_async_copy(room.at[i], out_ref.at[at_ref[i]], out_of.at[i]) for i in range(len(pieces))]
    for copy in first:
        copy.start()
    for one, two in zip(first, second):
        one.wait()
        two.start()
    for copy in second:
        copy.wait()


def assemble(pieces, at):
    anywhere = pl.BlockSpec(memory_space=pl.ANY)
    shape, dtype, count = pieces[0].shape, pieces[0].dtype, len(pieces)
    return pl.pallas_call(
        assemble_kernel,
        grid_spec=pltpu.PrefetchScalarGridSpec(
            num_scalar_prefetch=1,
            grid=(1,),
            in_specs=[anywhere] * count,
            out_specs=anywhere,
            scratch_shapes=[
                pltpu.VMEM((count,) + shape, dtype),
                pltpu.SemaphoreType.DMA((count,)),
                pltpu.SemaphoreType.DMA((count,)),
            ],
        ),
        out_shape=jax.ShapeDtypeStruct((count,) + shape, dtype),
        compiler_params=pltpu.CompilerParams(vmem_limit_bytes=48 << 20),
        name="assemble",
    )(at, *pieces)


def bias_sum_kernel(pairs_ref, row_ref, out_ref, *, own, rows):
    reach = 2 * REACH + 1
    lane = lax.broadcasted_iota(jnp.int32, (GRID, own), 1)
    query_row, query_col = lane // GRID, lane % GRID
    col_diff = lax.broadcasted_iota(jnp.int32, (GRID, own), 0) - query_col
    zero = jnp.zeros((GRID, own), jnp.float32)
    by_row = [zero] * reach
    for b in range(rows):
        block = pairs_ref[0, b * GRID : (b + 1) * GRID, :]
        row_diff = row_ref[b] - query_row
        for n in range(reach):
            by_row[n] = by_row[n] + jnp.where(row_diff == n - REACH, block, zero)
    for n in range(reach):
        for o in range(reach):
            kept = jnp.where(col_diff == o - REACH, by_row[n], zero)
            out_ref[0, n * reach + o, :] = jnp.sum(kept, axis=0)


def bias_sum(pairs, key_rows, own_rows):
    reach = 2 * REACH + 1
    rows = key_rows.shape[0]
    own, total = own_rows * GRID, rows * GRID
    block = pl.BlockSpec((1, total, own), lambda h: (h, 0, 0))
    by_lane = pl.pallas_call(
        functools.partial(bias_sum_kernel, own=own, rows=rows),
        grid=(HEADS,),
        in_specs=[block, pl.BlockSpec(memory_space=pltpu.SMEM)],
        out_specs=pl.BlockSpec((1, reach * reach, own), lambda h: (h, 0, 0)),
        out_shape=jax.ShapeDtypeStruct((HEADS, reach * reach, own), jnp.float32),
        name="bias_sum",
    )(pairs, key_rows)
    return jnp.sum(by_lane, axis=-1).reshape(HEADS, reach, reach)


def attend_kernel(mixed_ref, table_ref, *refs, own, total):
    out_ref, acc_ref = refs[-2:]

    def columns(part, low, high, count):
        block = mixed_ref[0, : count // GRID, 0, :, part * D + low : part * D + high]
        return block.reshape(count, high - low)

    for head in range(HEADS):
        low, high = head_window(head)
        query = columns(0, low, high, own) * head_mask(head, jnp.bfloat16)
        scores = nt_dot(columns(1, low, high, total), query) * score_scale + table_ref[head]
        top = jnp.max(scores, axis=0, keepdims=True)
        weight = jnp.exp(scores - top)
        weight = weight * (1.0 / jnp.sum(weight, axis=0, keepdims=True))
        result = tn_dot(weight.astype(jnp.bfloat16), columns(2, low, high, total))
        if head * HEAD_DIM % LANES == 0:
            acc_ref[:, low:high] = result
        else:
            mine = head_mask(head, jnp.float32)
            earlier = acc_ref[:, low : low + LANES]
            acc_ref[:, low : low + LANES] = jnp.where(mine[:, :LANES] > 0, result[:, :LANES], earlier)
            if high - low > LANES:
                acc_ref[:, low + LANES : high] = result[:, LANES:]
    out_ref[0, :, 0] = acc_ref[...].astype(jnp.bfloat16).reshape(own // GRID, GRID, D)


def attend_back_kernel(mixed_ref, grad_ref, table_ref, out_ref, bias_ref, q_ref, k_ref, v_ref, *, own, total):
    @pl.when((pl.program_id(0) == 0) & (pl.program_id(1) == 0))
    def _():
        bias_ref[...] = jnp.zeros_like(bias_ref)

    def columns(part, low, high, count):
        block = mixed_ref[0, : count // GRID, 0, :, part * D + low : part * D + high]
        return block.reshape(count, high - low)

    def put(ref, low, high, value, fresh):
        if fresh:
            ref[:, low:high] = value
        else:
            ref[:, low : low + LANES] += value[:, :LANES]
            if high - low > LANES:
                ref[:, low + LANES : high] = value[:, LANES:]

    for head in range(HEADS):
        low, high = head_window(head)
        fresh = head * HEAD_DIM % LANES == 0
        keep = head_mask(head, jnp.bfloat16)
        query = columns(0, low, high, own) * keep
        grad = grad_ref[0, :, 0, :, low:high].reshape(own, high - low) * keep
        keys = columns(1, low, high, total)
        scores = nt_dot(keys, query) * score_scale + table_ref[head]
        top = jnp.max(scores, axis=0, keepdims=True)
        weight = jnp.exp(scores - top)
        weight = weight * (1.0 / jnp.sum(weight, axis=0, keepdims=True))
        grad_weight = nt_dot(columns(2, low, high, total), grad)
        delta = jnp.sum(weight * grad_weight, axis=0, keepdims=True)
        grad_scores = weight * (grad_weight - delta)
        bias_ref[head] += grad_scores
        grad_low = grad_scores.astype(jnp.bfloat16)
        put(v_ref, low, high, low_dot(weight.astype(jnp.bfloat16), grad), fresh)
        put(k_ref, low, high, low_dot(grad_low, query), fresh)
        put(q_ref, low, high, tn_dot(grad_low, keys) * head_mask(head, jnp.float32), fresh)
    rows, own_rows = total // GRID, own // GRID
    out_ref[0, :own_rows, 0, :, :D] = (q_ref[...] * score_scale).astype(jnp.bfloat16).reshape(own_rows, GRID, D)
    if rows > own_rows:
        out_ref[0, own_rows:, 0, :, :D] = jnp.zeros((rows - own_rows, GRID, D), jnp.bfloat16)
    out_ref[0, :, 0, :, D : 2 * D] = (k_ref[...] * score_scale).astype(jnp.bfloat16).reshape(rows, GRID, D)
    out_ref[0, :, 0, :, 2 * D :] = v_ref[...].astype(jnp.bfloat16).reshape(rows, GRID, D)


def attend(mixed, table, kept, first, count, own_rows):
    seqs, rows = mixed.shape[:2]
    own, total = own_rows * GRID, rows * GRID
    kept = () if kept is None else (kept,)
    return pl.pallas_call(
        functools.partial(attend_kernel, own=own, total=total),
        grid=(count, PACK),
        in_specs=[
            pl.BlockSpec((1, rows, 1, GRID, 3 * D), lambda s, p: (first + s, 0, p, 0, 0)),
            pl.BlockSpec((HEADS, total, own), lambda s, p: (0, 0, 0)),
        ]
        + [pl.BlockSpec(memory_space=pl.ANY)] * len(kept),
        out_specs=pl.BlockSpec((1, own_rows, 1, GRID, D), lambda s, p: (first + s, 0, p, 0, 0)),
        out_shape=jax.ShapeDtypeStruct((seqs, own_rows, PACK, GRID, D), jnp.bfloat16),
        scratch_shapes=[pltpu.VMEM((own, D), jnp.float32)],
        input_output_aliases={2: 0} if kept else {},
        compiler_params=pltpu.CompilerParams(
            dimension_semantics=("arbitrary", "arbitrary"), vmem_limit_bytes=48 << 20
        ),
        name="attend",
    )(mixed, table, *kept)


def attend_back(mixed, grad, table, own_rows):
    seqs, rows = mixed.shape[:2]
    own, total = own_rows * GRID, rows * GRID
    return pl.pallas_call(
        functools.partial(attend_back_kernel, own=own, total=total),
        grid=(seqs, PACK),
        in_specs=[
            pl.BlockSpec((1, rows, 1, GRID, 3 * D), lambda s, p: (s, 0, p, 0, 0)),
            pl.BlockSpec((1, own_rows, 1, GRID, D), lambda s, p: (s, 0, p, 0, 0)),
            pl.BlockSpec((HEADS, total, own), lambda s, p: (0, 0, 0)),
        ],
        out_specs=[
            pl.BlockSpec((1, rows, 1, GRID, 3 * D), lambda s, p: (s, 0, p, 0, 0)),
            pl.BlockSpec((HEADS, total, own), lambda s, p: (0, 0, 0)),
        ],
        out_shape=[
            jax.ShapeDtypeStruct((seqs, rows, PACK, GRID, 3 * D), jnp.bfloat16),
            jax.ShapeDtypeStruct((HEADS, total, own), jnp.float32),
        ],
        scratch_shapes=[
            pltpu.VMEM((own, D), jnp.float32),
            pltpu.VMEM((total, D), jnp.float32),
            pltpu.VMEM((total, D), jnp.float32),
        ],
        compiler_params=pltpu.CompilerParams(
            dimension_semantics=("arbitrary", "arbitrary"), vmem_limit_bytes=48 << 20
        ),
        name="attend_back",
    )(mixed, grad, table)


def trade(block, axis, bit):
    size = lax.axis_size(axis)
    return lax.ppermute(block, axis, [(i, i ^ bit) for i in range(size)])


def sum_all(block):
    for axis in ("seq", "rows"):
        bit = 1
        while bit < lax.axis_size(axis):
            block = block + trade(block, axis, bit)
            bit *= 2
    return block


def gather_small(block):
    size = lax.axis_size("seq")
    place = lax.axis_index("seq")
    axis, bit = 0, size // 2
    while bit:
        got = trade(block, "seq", bit)
        upper = (place & bit) > 0
        block = jnp.stack([jnp.where(upper, got, block), jnp.where(upper, block, got)], axis=axis)
        axis, bit = axis + 1, bit // 2
    return block.reshape((size,) + block.shape[axis:])


def scatter_small(block):
    size = lax.axis_size("seq")
    place = lax.axis_index("seq")
    bit = 1
    while bit < size:
        block = block.reshape((block.shape[0] // 2, 2) + block.shape[1:])
        upper = (place & bit) > 0
        kept = jnp.where(upper, block[:, 1], block[:, 0])
        sent = jnp.where(upper, block[:, 0], block[:, 1])
        block = kept + trade(sent, "seq", bit)
        bit *= 2
    return block[0]


def gather_images(block):
    return gather_small(block.astype(jnp.bfloat16)).reshape(-1, block.shape[1])


def sum_rows(block):
    if lax.axis_size("rows") == 2:
        return block.astype(jnp.float32) + trade(block, "rows", 1).astype(jnp.float32)
    return lax.psum(block, "rows").astype(jnp.float32)


def after(value, *earlier):
    return lax.optimization_barrier((value,) + earlier)[0]


def ring_order(chips):
    return list(range(0, chips, 2)) + list(range(1, chips, 2))[::-1]


def ring_path(chips, step):
    order = ring_order(chips)
    return [(2 * order[i] + c, 2 * order[(i + step) % chips] + c) for i in range(chips) for c in range(2)]


def ring_spot(chips, chip):
    return jnp.where(chip % 2 == 0, chip // 2, chips - 1 - chip // 2)


def chip_at(chips, spot):
    spot = (spot + chips) % chips
    return jnp.where(spot < chips // 2, 2 * spot, 2 * chips - 1 - 2 * spot)


class RingGather:
    def __init__(self, shard):
        self.size = lax.axis_size("seq")
        self.chips = self.size // 2
        place = lax.axis_index("seq")
        self.core, self.chip = place % 2, place // 2
        self.spot = ring_spot(self.chips, self.chip)
        ahead = self.chips // 2
        self.hops = {1: ahead, -1: self.chips - 1 - ahead}
        self.moving = {1: shard, -1: shard}
        self.done = 0
        self.fresh = [(shard, self.chip)]
        self.pieces, self.at = [], []

    def steps(self):
        return [step for step in (1, -1) if self.done < self.hops[step]]

    def load(self):
        return tuple(self.moving[step] for step in self.steps()) + tuple(piece for piece, _ in self.fresh)

    def fly(self, loads):
        steps = self.steps()
        gots = tuple(
            lax.ppermute(block, "seq", ring_path(self.chips, step)) for block, step in zip(loads, steps)
        )
        return gots + tuple(trade(block, "seq", 1) for block in loads[len(steps) :])

    def land(self, loads, gots):
        steps = self.steps()
        self.done += 1
        for (piece, chip), other in zip(self.fresh, gots[len(steps) :]):
            self.pieces += [piece, other]
            self.at += [chip * 2 + self.core, chip * 2 + 1 - self.core]
        self.fresh = []
        for step, got in zip(steps, gots):
            self.moving[step] = got
            self.fresh.append((got, chip_at(self.chips, self.spot - step * self.done)))

    def whole(self):
        while self.fresh:
            slot([self], lambda: ())
        full = assemble(self.pieces, jnp.stack(self.at).astype(jnp.int32))
        return full.reshape(-1, full.shape[-1])


class RingScatter:
    def __init__(self, grad):
        self.size = lax.axis_size("seq")
        self.chips = self.size // 2
        place = lax.axis_index("seq")
        core, chip = place % 2, place // 2
        self.spot = ring_spot(self.chips, chip)
        low = grad.astype(jnp.bfloat16).reshape(self.chips, 2, grad.shape[0] // self.size, -1)
        self.kept = lax.dynamic_index_in_dim(low, core, 1, keepdims=False)
        self.sent = lax.dynamic_index_in_dim(low, 1 - core, 1, keepdims=False)
        ahead = self.chips // 2
        self.hops = {1: ahead, -1: self.chips - 1 - ahead}
        self.stage = 0
        self.got = {}
        self.total = None

    def piece(self, offset):
        at = chip_at(self.chips, self.spot + offset)
        return lax.dynamic_index_in_dim(self.chip_sum, at, 0, keepdims=False).astype(jnp.float32)

    def steps(self):
        return [step for step in (1, -1) if self.stage <= self.hops[step]]

    def load(self):
        if self.stage == 0:
            return (self.sent,)
        if self.steps():
            loads = []
            for step in self.steps():
                moving = self.piece(step * (self.hops[step] - self.stage + 1))
                if self.stage > 1:
                    moving = moving + self.got[step].astype(jnp.float32)
                loads.append(moving.astype(jnp.bfloat16))
            return tuple(loads)
        total = self.piece(0)
        for got in self.got.values():
            total = total + got.astype(jnp.float32)
        return (total.astype(jnp.bfloat16),)

    def fly(self, loads):
        if self.stage == 0:
            return (trade(loads[0], "seq", 1),)
        if self.steps():
            return tuple(
                lax.ppermute(block, "seq", ring_path(self.chips, step)) for block, step in zip(loads, self.steps())
            )
        if lax.axis_size("rows") == 2:
            return (trade(loads[0], "rows", 1),)
        return (lax.psum(loads[0], "rows"),)

    def land(self, loads, gots):
        if self.stage == 0:
            both = self.kept.astype(jnp.float32) + gots[0].astype(jnp.float32)
            self.chip_sum = both.astype(jnp.bfloat16)
        elif self.steps():
            for step, got in zip(self.steps(), gots):
                self.got[step] = got
        else:
            self.total = gots[0].astype(jnp.float32)
            if lax.axis_size("rows") == 2:
                self.total = self.total + loads[0].astype(jnp.float32)
        self.stage += 1

    def whole(self):
        while self.total is None:
            slot([self], lambda: ())
        return self.total


class RowSum:
    def __init__(self, block):
        self.block = block
        self.total = None

    def load(self):
        return (self.block,)

    def fly(self, loads):
        if lax.axis_size("rows") == 2:
            return (trade(loads[0], "rows", 1),)
        return (lax.psum(loads[0], "rows"),)

    def land(self, loads, gots):
        self.total = gots[0].astype(jnp.float32)
        if lax.axis_size("rows") == 2:
            self.total = self.total + loads[0].astype(jnp.float32)


def slot(rings, work, *values, wait=()):
    loads = [ring.load() for ring in rings]
    held = lax.optimization_barrier(tuple(values) + sum(loads, ()))
    values, rest = held[: len(values)], held[len(values) :]
    gots = []
    for i, ring in enumerate(rings):
        loads[i], rest = rest[: len(loads[i])], rest[len(loads[i]) :]
        gots.append(ring.fly(loads[i]))
    results = tuple(work(*values))
    held = lax.optimization_barrier(results + tuple(wait) + sum(gots, ()))
    results, rest = held[: len(results)], held[len(results) + len(wait) :]
    for i, ring in enumerate(rings):
        got, rest = rest[: len(gots[i])], rest[len(gots[i]) :]
        ring.land(loads[i], got)
    return results + held[len(results) : len(results) + len(wait)]


def on_device(
    row_shards,
    tokens,
    image_ids,
    timestep,
    norm1_gain,
    norm1_shift,
    time_in_weight,
    time_in_bias,
    time_out_weight,
    time_out_bias,
    mix_weight,
    time_mix_weight,
    position_bias,
    proj_weight,
    proj_bias,
    norm2_gain,
    norm2_shift,
    up_weight,
    up_bias,
    down_weight,
    down_bias,
    cotangent,
):
    seq_rows, local_rows, columns, _ = tokens.shape
    act_tokens = tokens.reshape(seq_rows, local_rows, PACK, GRID, D)
    act_cot = cotangent.reshape(seq_rows, local_rows, PACK, GRID, D)
    token_count = seq_rows * local_rows * columns
    seqs = lax.axis_size("seq")
    place = lax.axis_index("seq")
    images = seqs * seq_rows * PACK
    width_part, freq_part = D // seqs, FREQ // seqs

    def my_part(array, part, axis):
        return lax.dynamic_slice_in_dim(array, place * part, part, axis=axis)

    full_mix = lax.all_gather(mix_weight, "seq", axis=0, tiled=True)
    borrowed, borrowed_at, sent_rows = borrow_rows(act_tokens, row_shards)
    timestep, time_in_weight = lax.optimization_barrier((timestep, time_in_weight, sent_rows))[:2]
    half_width = FREQ // 2
    frequency = jnp.exp(-math.log(10000.0) * jnp.arange(half_width, dtype=jnp.float32) / half_width)

    def time_first(timestep, time_in_weight):
        angles = timestep.astype(jnp.float32).reshape(-1, 1) * frequency
        features = jnp.concatenate([jnp.cos(angles), jnp.sin(angles)], axis=-1).astype(jnp.bfloat16)
        spare = -features.size % D
        features = jnp.pad(features.reshape(-1), (0, spare)).reshape(-1, D)
        both = gather_small(jnp.concatenate([time_in_weight, features], axis=0))
        full_tin = both[:, :freq_part].reshape(FREQ, D)
        features = both[:, freq_part:].reshape(seqs, -1)[:, : seq_rows * PACK * FREQ].reshape(images, FREQ)
        time_pre = jnp.einsum(
            "fd,if->di", my_part(full_tin, width_part, 1), features, preferred_element_type=jnp.float32
        )
        return (features, time_pre + my_part(time_in_bias, width_part, 0)[:, None])

    def time_second(time_pre):
        time_hidden = jax.nn.silu(time_pre).astype(jnp.bfloat16)
        partial = jnp.einsum("fd,fi->di", time_out_weight, time_hidden, preferred_element_type=jnp.float32)
        time_embed = scatter_small(partial.reshape(seqs, width_part, images))
        time_embed = time_embed + my_part(time_out_bias, width_part, 0)[:, None]
        return (time_hidden, time_embed.astype(jnp.bfloat16))

    def time_third(time_embed):
        partial = jnp.einsum("di,de->ie", time_embed, time_mix_weight, preferred_element_type=jnp.float32)
        return (scatter_small(partial.reshape(seqs, seq_rows * PACK, 3 * D)),)

    features, time_pre = time_first(timestep, time_in_weight)
    time_hidden, time_embed = time_second(time_pre)
    key_at = jnp.concatenate([jnp.arange(local_rows), borrowed_at])
    key_row = lax.axis_index("rows") * local_rows + key_at
    key_rows = jnp.where((key_row >= 0) & (key_row < GRID), key_at, 4 * GRID).astype(jnp.int32)
    table = bias_table(position_bias, key_rows, local_rows)
    time_embed = after(time_embed, table)
    (time_proj,) = time_third(time_embed)
    time_proj = time_proj.reshape(seq_rows, PACK, 3 * D)
    my_features = my_part(features, freq_part, 1)
    block_slots = image_ids[:, ::GRID]
    slot_hot = (block_slots[:, :, None] == jnp.arange(PACK, dtype=jnp.int32)[None, None, :]).astype(
        jnp.float32
    )
    unit_time = jnp.einsum("skp,spe->ske", slot_hot, time_proj, precision=highest)
    ext_tokens = jnp.concatenate([act_tokens, borrowed], axis=1)
    ext_rows = ext_tokens.shape[1]
    ext_count = seq_rows * ext_rows * columns

    normed1 = norm_forward(ext_tokens.astype(jnp.float32), norm1_gain, norm1_shift)[0].astype(jnp.bfloat16)
    full_proj = lax.all_gather(proj_weight, "seq", axis=0, tiled=True)
    full_down = lax.all_gather(down_weight, "seq", axis=0, tiled=True)
    up_ring = RingGather(after(up_weight, full_mix[:8, :128]))

    def to_mixed(normed1):
        return ((low_dot(normed1, full_mix) + unit_time[:, None, :, None, :]).astype(jnp.bfloat16),)

    (mixed,) = slot([up_ring], to_mixed, normed1)
    part = -(-seq_rows // 2)
    (attended,) = slot([up_ring], lambda mixed: (attend(mixed, table, None, 0, part, local_rows),), mixed)
    (attended,) = slot(
        [up_ring], lambda kept: (attend(mixed, table, kept, part, seq_rows - part, local_rows),), attended
    )

    flat_tokens = act_tokens.astype(jnp.float32)

    def second_norm(attended):
        residual = flat_tokens + low_dot(attended, full_proj) + proj_bias
        normed2, unit_two, inverse_two = norm_forward(residual, norm2_gain, norm2_shift)
        return (residual, normed2.astype(jnp.bfloat16), unit_two, inverse_two)

    residual, normed2, unit_two, inverse_two = slot([up_ring], second_norm, attended)
    full_up = up_ring.whole()
    hidden_pre = low_dot(normed2, full_up) + up_bias
    hidden = gelu_tanh(hidden_pre).astype(jnp.bfloat16)
    flat_hidden = hidden.reshape(token_count, FF)
    flat_cot = act_cot.reshape(token_count, D)
    grad_down_w = jnp.einsum("nf,nd->fd", flat_hidden, flat_cot, preferred_element_type=jnp.float32)
    grad_down_b = jnp.sum(flat_cot, axis=0, dtype=jnp.float32)
    down_part = lax.psum_scatter(grad_down_w.astype(jnp.bfloat16), "seq", scatter_dimension=0, tiled=True)
    grad_hidden = jnp.einsum(
        "nd,fd->nf", after(flat_cot, grad_down_w), full_down, preferred_element_type=jnp.float32
    )
    gelu_back = jax.vjp(gelu_tanh, hidden_pre.reshape(token_count, FF))[1]
    grad_pre = gelu_back(grad_hidden)[0].astype(jnp.bfloat16)
    flat_normed2 = normed2.reshape(token_count, D)
    grad_up_w = jnp.einsum("nd,nf->df", flat_normed2, grad_pre, preferred_element_type=jnp.float32)
    grad_up_b = jnp.sum(grad_pre, axis=0, dtype=jnp.float32)
    up_part = lax.psum_scatter(grad_up_w.astype(jnp.bfloat16), "seq", scatter_dimension=0, tiled=True)

    def back_up(grad_pre):
        grad_normed2 = jnp.einsum("nf,df->nd", grad_pre, full_up, preferred_element_type=jnp.float32)
        return (grad_normed2.reshape(act_tokens.shape),)

    def back_norm(grad_normed2):
        grad_norm_two, grad_gain_two, grad_shift_two = norm_backward(
            grad_normed2, unit_two, inverse_two, norm2_gain
        )
        grad_residual = act_cot.astype(jnp.float32) + grad_norm_two
        grad_branch = grad_residual.astype(jnp.bfloat16).reshape(token_count, D)
        grad_proj_w = jnp.einsum(
            "nd,ne->de", attended.reshape(token_count, D), grad_branch, preferred_element_type=jnp.float32
        ).astype(jnp.bfloat16)
        grad_proj_b = jnp.sum(grad_branch, axis=0, dtype=jnp.float32)
        grad_attended = jnp.einsum(
            "ne,de->nd", grad_branch, full_proj, preferred_element_type=jnp.float32
        ).astype(jnp.bfloat16)
        grad_attended = grad_attended.reshape(act_tokens.shape)
        return (grad_residual, grad_gain_two, grad_shift_two, grad_proj_w, grad_proj_b, grad_attended)

    (grad_normed2,) = back_up(after(grad_pre, grad_up_w))
    (grad_residual, grad_gain_two, grad_shift_two, grad_proj_w, grad_proj_b, grad_attended) = back_norm(grad_normed2)
    proj_part = lax.psum_scatter(grad_proj_w, "seq", scatter_dimension=0, tiled=True)
    grad_mixed, grad_table = attend_back(mixed, after(grad_attended, grad_proj_w), table, local_rows)
    down_sum = RowSum(down_part)

    def weight_mix(grad_mixed):
        grad_mix_w = jnp.einsum(
            "nd,ne->de",
            normed1.reshape(ext_count, D),
            grad_mixed.reshape(ext_count, 3 * D),
            preferred_element_type=jnp.float32,
        )
        grad_unit = sum_rows(jnp.sum(grad_mixed, axis=(1, 3), dtype=jnp.float32))
        grad_time_proj = jnp.einsum("skp,ske->spe", slot_hot, grad_unit, precision=highest)
        return (grad_mix_w.astype(jnp.bfloat16), grad_time_proj.reshape(-1, 3 * D))

    def back_mixed(grad_mixed, grad_time_proj):
        grad_in = jnp.einsum(
            "ne,de->nd", grad_mixed.reshape(ext_count, 3 * D), full_mix, preferred_element_type=jnp.float32
        ).reshape(ext_tokens.shape)
        return (
            grad_in[:, :local_rows],
            grad_in[:, local_rows:].astype(jnp.bfloat16),
            after(lax.all_gather(grad_time_proj, "seq", axis=0, tiled=True)).astype(jnp.bfloat16),
        )

    def last_part(flat_hidden, grad_time_proj):
        output = (residual + low_dot(flat_hidden, full_down).reshape(residual.shape) + down_bias).astype(jnp.bfloat16)
        sum_tmix = low_dot(time_embed, grad_time_proj)
        grad_embed = jnp.einsum("de,ie->di", time_mix_weight, grad_time_proj, preferred_element_type=jnp.float32)
        return (output, sum_tmix, gather_images(grad_embed))

    def back_time(grad_embed, grad_table):
        bias_grad = bias_sum(grad_table, key_rows, local_rows)
        tout_bias = jnp.sum(grad_embed, axis=1, dtype=jnp.float32)
        sum_tout = jnp.einsum("fi,di->fd", time_hidden, grad_embed, preferred_element_type=jnp.float32)
        grad_thidden = low_dot(time_out_weight, grad_embed)
        silu_back = jax.vjp(jax.nn.silu, time_pre)[1]
        grad_tpre = gather_images(silu_back(grad_thidden)[0])
        return (bias_grad, sum_tout, tout_bias, grad_tpre)

    grad_mix_w, grad_time_proj = slot([down_sum], weight_mix, grad_mixed)
    mix_sum = RingScatter(grad_mix_w)
    grad_own_in, grad_borrowed_in, grad_time_proj = slot([mix_sum], back_mixed, grad_mixed, grad_time_proj)
    grad_normed1 = return_rows(grad_own_in, grad_borrowed_in, row_shards)
    output, sum_tmix, grad_embed = slot([mix_sum], last_part, flat_hidden, grad_time_proj)
    up_sum, proj_sum = RowSum(up_part), RowSum(proj_part)
    bias_grad, sum_tout, tout_bias, grad_tpre = slot([mix_sum, up_sum], back_time, grad_embed, grad_table)

    def back_first(grad_normed1, grad_tpre):
        _, unit_one, inverse_one = norm_forward(act_tokens.astype(jnp.float32), norm1_gain, norm1_shift)
        grad_norm_one, grad_gain_one, grad_shift_one = norm_backward(
            grad_normed1, unit_one, inverse_one, norm1_gain
        )
        tin_bias = jnp.sum(grad_tpre, axis=1, dtype=jnp.float32)
        sum_tin = jnp.einsum(
            "if,di->fd", my_features, grad_tpre, preferred_element_type=jnp.float32
        )
        tokens_grad = (grad_residual + grad_norm_one).astype(jnp.bfloat16)
        return (tokens_grad, grad_gain_one, grad_shift_one, sum_tin, tin_bias)

    tokens_grad, grad_gain_one, grad_shift_one, sum_tin, tin_bias = slot(
        [mix_sum, proj_sum], back_first, grad_normed1, grad_tpre
    )
    small = (
        grad_gain_one,
        grad_shift_one,
        bias_grad,
        grad_proj_b,
        grad_gain_two,
        grad_shift_two,
        grad_up_b,
        grad_down_b,
    )
    (flat,) = slot([mix_sum], lambda *parts: (sum_all(jnp.concatenate([p.reshape(-1) for p in parts])),), *small)
    sum_down, sum_up, sum_proj, sum_mix = down_sum.total, up_sum.total, proj_sum.total, mix_sum.whole()
    ends = [0]
    for part in small:
        ends.append(ends[-1] + part.size)
    (gain_one, shift_one, bias_total, proj_total, gain_two, shift_two, up_total, down_total) = (
        flat[first:last].reshape(part.shape) for first, last, part in zip(ends, ends[1:], small)
    )
    output = output.reshape(tokens.shape)
    tokens_grad = tokens_grad.reshape(tokens.shape)
    return (
        output,
        tokens_grad,
        gain_one,
        shift_one,
        sum_tin,
        tin_bias,
        sum_tout,
        tout_bias,
        sum_mix,
        sum_tmix,
        bias_total,
        sum_proj,
        proj_total,
        gain_two,
        shift_two,
        sum_up,
        up_total,
        sum_down,
        down_total,
    )


def solution(mesh):
    whole, sharded = (P(), P("seq", None))
    acts = P("seq", "rows", None, None)
    return jax.shard_map(
        functools.partial(on_device, mesh.shape["rows"]),
        mesh=mesh,
        in_specs=(
            acts,
            sharded,
            sharded,
            whole,
            whole,
            sharded,
            whole,
            sharded,
            whole,
            sharded,
            sharded,
            whole,
            sharded,
            whole,
            whole,
            whole,
            sharded,
            whole,
            sharded,
            whole,
            acts,
        ),
        out_specs=(
            acts,
            acts,
            whole,
            whole,
            sharded,
            whole,
            sharded,
            whole,
            sharded,
            sharded,
            whole,
            sharded,
            whole,
            whole,
            whole,
            sharded,
            whole,
            sharded,
            whole,
        ),
        check_vma=False,
    )
```

```python
import functools
import math

import jax
import jax.numpy as jnp
from jax import lax
from jax.experimental import pallas as pl
from jax.experimental.pallas import tpu as pltpu
from jax.sharding import PartitionSpec as P

D = 1152
HEADS = 16
HEAD_DIM = 72
FF = 4608
FREQ = 256
GRID = 16
PACK = 4
REACH = 4
LANES = 128


epsilon = 1e-06
floor_score = -1e30
highest = lax.Precision.HIGHEST
score_scale = HEAD_DIM ** (-0.5)


def low_dot(left, right):
    return jnp.dot(left, right, preferred_element_type=jnp.float32)


def norm_forward(values, norm_gain, norm_shift):
    centred = values - jnp.mean(values, axis=-1, keepdims=True)
    inverse = lax.rsqrt(jnp.mean(centred * centred, axis=-1, keepdims=True) + epsilon)
    unit_rows = centred * inverse
    return (unit_rows * norm_gain + norm_shift, unit_rows, inverse)


def norm_backward(grad_out, unit_rows, inverse, norm_gain):
    scaled = grad_out * norm_gain
    grad_in = inverse * (
        scaled
        - jnp.mean(scaled, axis=-1, keepdims=True)
        - unit_rows * jnp.mean(scaled * unit_rows, axis=-1, keepdims=True)
    )
    leading = tuple(range(grad_out.ndim - 1))
    return (grad_in, jnp.sum(grad_out * unit_rows, axis=leading), jnp.sum(grad_out, axis=leading))


def row_plan(local_rows, shards):
    if shards == 2 and local_rows >= REACH:
        return (True, 1, REACH)
    sent = min(local_rows, REACH)
    return (False, -(-REACH // local_rows), sent)


def route(shards, distance):
    return [(i - distance, i) for i in range(shards) if 0 <= i - distance < shards]


def borrow_rows(own, shards):
    rows = own.shape[1]
    one_sided, turns, sent = row_plan(rows, shards)
    place = lax.axis_index("rows")
    if one_sided:
        start = jnp.where(place == 0, rows - sent, 0)
        block = lax.dynamic_slice_in_dim(own, start, sent, axis=1)
        got = lax.ppermute(block, "rows", [(0, 1), (1, 0)])
        first = jnp.where(place == 0, rows, -sent)
        return (got, first + jnp.arange(sent), block)
    pieces, where = [], []
    for turn in range(turns, 0, -1):
        pieces.append(lax.ppermute(own[:, rows - sent :], "rows", route(shards, turn)))
        where.append(jnp.arange(sent) - (turn - 1) * rows - sent)
    for turn in range(1, turns + 1):
        pieces.append(lax.ppermute(own[:, :sent], "rows", route(shards, -turn)))
        where.append(jnp.arange(sent) + turn * rows)
    return (jnp.concatenate(pieces, axis=1), jnp.concatenate(where), own[:, :sent])


def head_window(head):
    first, last = head * HEAD_DIM, (head + 1) * HEAD_DIM
    return (first // LANES * LANES, -(-last // LANES) * LANES)


def head_mask(head, dtype):
    low, high = head_window(head)
    lane = lax.broadcasted_iota(jnp.int32, (1, high - low), 1) + low
    return ((lane >= head * HEAD_DIM) & (lane < (head + 1) * HEAD_DIM)).astype(dtype)


def nt_dot(left, right):
    return lax.dot_general(left, right, (((1,), (1,)), ((), ())), preferred_element_type=jnp.float32)


def tn_dot(left, right):
    return lax.dot_general(left, right, (((0,), (0,)), ((), ())), preferred_element_type=jnp.float32)


def table_kernel(bias_ref, row_ref, out_ref, *, own, rows):
    head = pl.program_id(0)
    reach = 2 * REACH + 1
    lane = lax.broadcasted_iota(jnp.int32, (GRID, own), 1)
    query_row, query_col = lane // GRID, lane % GRID
    col_diff = lax.broadcasted_iota(jnp.int32, (GRID, own), 0) - query_col
    floor = jnp.full((GRID, own), floor_score, jnp.float32)
    by_row = []
    for n in range(reach):
        value = floor
        for o in range(reach):
            value = jnp.where(col_diff == o - REACH, bias_ref[head, n * reach + o], value)
        by_row.append(value)
    for b in range(rows):
        row_diff = row_ref[b] - query_row
        value = floor
        for n in range(reach):
            value = jnp.where(row_diff == n - REACH, by_row[n], value)
        out_ref[0, b * GRID : (b + 1) * GRID, :] = value


def bias_table(position_bias, key_rows, own_rows):
    rows = key_rows.shape[0]
    own, total = own_rows * GRID, rows * GRID
    smem = pl.BlockSpec(memory_space=pltpu.SMEM)
    return pl.pallas_call(
        functools.partial(table_kernel, own=own, rows=rows),
        grid=(HEADS,),
        in_specs=[smem, smem],
        out_specs=pl.BlockSpec((1, total, own), lambda h: (h, 0, 0)),
        out_shape=jax.ShapeDtypeStruct((HEADS, total, own), jnp.float32),
        name="bias_table",
    )(position_bias.reshape(HEADS, -1), key_rows)


def assemble_kernel(at_ref, *refs, count):
    pieces, out_ref, room, into, out_of = refs[:count], refs[-4], refs[-3], refs[-2], refs[-1]
    first = [pltpu.make_async_copy(piece, room.at[i], into.at[i]) for i, piece in enumerate(pieces)]
    second = [pltpu.make_async_copy(room.at[i], out_ref.at[at_ref[i]], out_of.at[i]) for i in range(len(pieces))]
    for copy in first:
        copy.start()
    for one, two in zip(first, second):
        one.wait()
        two.start()
    for copy in second:
        copy.wait()


def assemble(pieces, at, size, kept=None):
    anywhere = pl.BlockSpec(memory_space=pl.ANY)
    shape, dtype, count = pieces[0].shape, pieces[0].dtype, len(pieces)
    return pl.pallas_call(
        functools.partial(assemble_kernel, count=len(pieces)),
        grid_spec=pltpu.PrefetchScalarGridSpec(
            num_scalar_prefetch=1,
            grid=(1,),
            in_specs=[anywhere] * (count if kept is None else count + 1),
            out_specs=anywhere,
            scratch_shapes=[
                pltpu.VMEM((count,) + shape, dtype),
                pltpu.SemaphoreType.DMA((count,)),
                pltpu.SemaphoreType.DMA((count,)),
            ],
        ),
        out_shape=jax.ShapeDtypeStruct((size,) + shape, dtype),
        input_output_aliases={} if kept is None else {count + 1: 0},
        compiler_params=pltpu.CompilerParams(vmem_limit_bytes=48 << 20),
        name="assemble",
    )(at, *pieces, *(() if kept is None else (kept,)))


def bias_sum_kernel(*refs, own, rows):
    pair_refs, row_ref, out_ref = refs[:-2], refs[-2], refs[-1]
    reach = 2 * REACH + 1
    lane = lax.broadcasted_iota(jnp.int32, (GRID, own), 1)
    query_row, query_col = lane // GRID, lane % GRID
    col_diff = lax.broadcasted_iota(jnp.int32, (GRID, own), 0) - query_col
    zero = jnp.zeros((GRID, own), jnp.float32)
    for head in range(out_ref.shape[0]):
        by_row = [zero] * reach
        for b in range(rows):
            block = sum(pairs[head, b * GRID : (b + 1) * GRID, :] for pairs in pair_refs)
            row_diff = row_ref[b] - query_row
            for n in range(reach):
                by_row[n] = by_row[n] + jnp.where(row_diff == n - REACH, block, zero)
        for n in range(reach):
            for o in range(reach):
                kept = jnp.where(col_diff == o - REACH, by_row[n], zero)
                out_ref[head, n * reach + o, :] = jnp.sum(kept, axis=0)


def bias_sum(pairs, key_rows, own_rows):
    reach = 2 * REACH + 1
    rows = key_rows.shape[0]
    own, total = own_rows * GRID, rows * GRID
    heads = 4
    block = pl.BlockSpec((heads, total, own), lambda h: (h, 0, 0))
    by_lane = pl.pallas_call(
        functools.partial(bias_sum_kernel, own=own, rows=rows),
        grid=(HEADS // heads,),
        in_specs=[block] * len(pairs) + [pl.BlockSpec(memory_space=pltpu.SMEM)],
        out_specs=pl.BlockSpec((heads, reach * reach, own), lambda h: (h, 0, 0)),
        out_shape=jax.ShapeDtypeStruct((HEADS, reach * reach, own), jnp.float32),
        name="bias_sum",
    )(*pairs, key_rows)
    return jnp.sum(by_lane, axis=-1).reshape(HEADS, reach, reach)


def attend_kernel(mixed_ref, table_ref, out_ref, acc_ref, *, own, total):
    def columns(part, low, high, count):
        block = mixed_ref[0, : count // GRID, 0, :, part * D + low : part * D + high]
        return block.reshape(count, high - low)

    for head in range(HEADS):
        low, high = head_window(head)
        query = columns(0, low, high, own) * head_mask(head, jnp.bfloat16)
        scores = nt_dot(columns(1, low, high, total), query) * score_scale + table_ref[head]
        top = jnp.max(scores, axis=0, keepdims=True)
        weight = jnp.exp(scores - top)
        weight = weight * (1.0 / jnp.sum(weight, axis=0, keepdims=True))
        result = tn_dot(weight.astype(jnp.bfloat16), columns(2, low, high, total))
        if head * HEAD_DIM % LANES == 0:
            acc_ref[:, low:high] = result
        else:
            mine = head_mask(head, jnp.float32)
            earlier = acc_ref[:, low : low + LANES]
            acc_ref[:, low : low + LANES] = jnp.where(mine[:, :LANES] > 0, result[:, :LANES], earlier)
            if high - low > LANES:
                acc_ref[:, low + LANES : high] = result[:, LANES:]
    out_ref[0, :, 0] = acc_ref[...].astype(jnp.bfloat16).reshape(own // GRID, GRID, D)


def attend_back_kernel(mixed_ref, grad_ref, table_ref, *refs, own, total):
    out_ref, bias_ref, unit_ref, q_ref, k_ref, v_ref = refs[-6:]

    @pl.when((pl.program_id(0) == 0) & (pl.program_id(1) == 0))
    def _():
        bias_ref[...] = jnp.zeros_like(bias_ref)

    def columns(part, low, high, count):
        block = mixed_ref[0, : count // GRID, 0, :, part * D + low : part * D + high]
        return block.reshape(count, high - low)

    def put(ref, low, high, value, fresh):
        if fresh:
            ref[:, low:high] = value
        else:
            ref[:, low : low + LANES] += value[:, :LANES]
            if high - low > LANES:
                ref[:, low + LANES : high] = value[:, LANES:]

    for head in range(HEADS):
        low, high = head_window(head)
        fresh = head * HEAD_DIM % LANES == 0
        keep = head_mask(head, jnp.bfloat16)
        query = columns(0, low, high, own) * keep
        grad = grad_ref[0, :, 0, :, low:high].reshape(own, high - low) * keep
        keys = columns(1, low, high, total)
        scores = nt_dot(keys, query) * score_scale + table_ref[head]
        top = jnp.max(scores, axis=0, keepdims=True)
        weight = jnp.exp(scores - top)
        weight = weight * (1.0 / jnp.sum(weight, axis=0, keepdims=True))
        grad_weight = nt_dot(columns(2, low, high, total), grad)
        delta = jnp.sum(weight * grad_weight, axis=0, keepdims=True)
        grad_scores = weight * (grad_weight - delta)
        bias_ref[head] += grad_scores
        grad_low = grad_scores.astype(jnp.bfloat16)
        put(v_ref, low, high, low_dot(weight.astype(jnp.bfloat16), grad), fresh)
        put(k_ref, low, high, low_dot(grad_low, query), fresh)
        put(q_ref, low, high, tn_dot(grad_low, keys) * head_mask(head, jnp.float32), fresh)
    rows, own_rows = total // GRID, own // GRID
    out_ref[0, :own_rows, 0, :, :D] = (q_ref[...] * score_scale).astype(jnp.bfloat16).reshape(own_rows, GRID, D)
    if rows > own_rows:
        out_ref[0, own_rows:, 0, :, :D] = jnp.zeros((rows - own_rows, GRID, D), jnp.bfloat16)
    out_ref[0, :, 0, :, D : 2 * D] = (k_ref[...] * score_scale).astype(jnp.bfloat16).reshape(rows, GRID, D)
    out_ref[0, :, 0, :, 2 * D :] = v_ref[...].astype(jnp.bfloat16).reshape(rows, GRID, D)
    slot_at = pl.program_id(1)
    for part, ref, scale in ((0, q_ref, score_scale), (1, k_ref, score_scale), (2, v_ref, 1.0)):
        low = (ref[...] * scale).astype(jnp.bfloat16).astype(jnp.float32)
        unit_ref[0, pl.ds(slot_at, 1), part * D : (part + 1) * D] = jnp.sum(low, axis=0, keepdims=True)


def attend(mixed, table, own_rows):
    seqs, rows = mixed.shape[:2]
    own, total = own_rows * GRID, rows * GRID
    return pl.pallas_call(
        functools.partial(attend_kernel, own=own, total=total),
        grid=(seqs, PACK),
        in_specs=[
            pl.BlockSpec((1, rows, 1, GRID, 3 * D), lambda s, p: (s, 0, p, 0, 0)),
            pl.BlockSpec((HEADS, total, own), lambda s, p: (0, 0, 0)),
        ],
        out_specs=pl.BlockSpec((1, own_rows, 1, GRID, D), lambda s, p: (s, 0, p, 0, 0)),
        out_shape=jax.ShapeDtypeStruct((seqs, own_rows, PACK, GRID, D), jnp.bfloat16),
        scratch_shapes=[pltpu.VMEM((own, D), jnp.float32)],
        compiler_params=pltpu.CompilerParams(
            dimension_semantics=("arbitrary", "arbitrary"), vmem_limit_bytes=48 << 20
        ),
        name="attend",
    )(mixed, table)


def attend_back(mixed, grad, table, kept, span, own_rows):
    seqs, rows = mixed.shape[:2]
    own, total = own_rows * GRID, rows * GRID
    first = span.start
    kept = () if kept is None else (kept,)
    return pl.pallas_call(
        functools.partial(attend_back_kernel, own=own, total=total),
        grid=(span.stop - span.start, PACK),
        in_specs=[
            pl.BlockSpec((1, rows, 1, GRID, 3 * D), lambda s, p: (first + s, 0, p, 0, 0)),
            pl.BlockSpec((1, own_rows, 1, GRID, D), lambda s, p: (first + s, 0, p, 0, 0)),
            pl.BlockSpec((HEADS, total, own), lambda s, p: (0, 0, 0)),
        ]
        + [pl.BlockSpec(memory_space=pl.ANY)] * len(kept),
        out_specs=[
            pl.BlockSpec((1, rows, 1, GRID, 3 * D), lambda s, p: (first + s, 0, p, 0, 0)),
            pl.BlockSpec((HEADS, total, own), lambda s, p: (0, 0, 0)),
            pl.BlockSpec((1, PACK, 3 * D), lambda s, p: (s, 0, 0)),
        ],
        out_shape=[
            jax.ShapeDtypeStruct((seqs, rows, PACK, GRID, 3 * D), jnp.bfloat16),
            jax.ShapeDtypeStruct((HEADS, total, own), jnp.float32),
            jax.ShapeDtypeStruct((span.stop - span.start, PACK, 3 * D), jnp.float32),
        ],
        scratch_shapes=[
            pltpu.VMEM((own, D), jnp.float32),
            pltpu.VMEM((total, D), jnp.float32),
            pltpu.VMEM((total, D), jnp.float32),
        ],
        input_output_aliases={3: 0} if kept else {},
        compiler_params=pltpu.CompilerParams(
            dimension_semantics=("arbitrary", "arbitrary"), vmem_limit_bytes=48 << 20
        ),
        name="attend_back",
    )(mixed, grad, table, *kept)


def trade(block, axis, bit):
    size = lax.axis_size(axis)
    return lax.ppermute(block, axis, [(i, i ^ bit) for i in range(size)])


def gather_small(block):
    size = lax.axis_size("seq")
    place = lax.axis_index("seq")
    axis, bit = 0, size // 2
    while bit:
        got = trade(block, "seq", bit)
        upper = (place & bit) > 0
        block = jnp.stack([jnp.where(upper, got, block), jnp.where(upper, block, got)], axis=axis)
        axis, bit = axis + 1, bit // 2
    return block.reshape((size,) + block.shape[axis:])


def scatter_small(block):
    size = lax.axis_size("seq")
    place = lax.axis_index("seq")
    bit = 1
    while bit < size:
        block = block.reshape((block.shape[0] // 2, 2) + block.shape[1:])
        upper = (place & bit) > 0
        kept = jnp.where(upper, block[:, 1], block[:, 0])
        sent = jnp.where(upper, block[:, 0], block[:, 1])
        block = kept + trade(sent, "seq", bit)
        bit *= 2
    return block[0]


def after(value, *earlier):
    return lax.optimization_barrier((value,) + earlier)[0]


def ring_order(chips):
    return list(range(0, chips, 2)) + list(range(1, chips, 2))[::-1]


def ring_path(chips, step):
    order = ring_order(chips)
    return [(2 * order[i] + c, 2 * order[(i + step) % chips] + c) for i in range(chips) for c in range(2)]


def ring_spot(chips, chip):
    return jnp.where(chip % 2 == 0, chip // 2, chips - 1 - chip // 2)


def chip_at(chips, spot):
    spot = (spot + chips) % chips
    return jnp.where(spot < chips // 2, 2 * spot, 2 * chips - 1 - 2 * spot)


class RingGather:
    def __init__(self, shard):
        self.size = lax.axis_size("seq")
        self.chips = self.size // 2
        place = lax.axis_index("seq")
        self.core, self.chip = place % 2, place // 2
        self.spot = ring_spot(self.chips, self.chip)
        ahead = self.chips // 2
        self.hops = {1: ahead, -1: self.chips - 1 - ahead}
        self.moving = {1: shard, -1: shard}
        self.done = 0
        self.fresh = [(shard, self.chip)]
        self.pieces, self.at = [], []
        self.full = None

    def place_pieces(self):
        self.full = assemble(self.pieces, jnp.stack(self.at).astype(jnp.int32), self.size, self.full)
        self.pieces, self.at = [], []

    def steps(self):
        return [step for step in (1, -1) if self.done < self.hops[step]]

    def load(self):
        return tuple(self.moving[step] for step in self.steps()) + tuple(piece for piece, _ in self.fresh)

    def fly(self, loads):
        steps = self.steps()
        gots = tuple(
            lax.ppermute(block, "seq", ring_path(self.chips, step)) for block, step in zip(loads, steps)
        )
        return gots + tuple(trade(block, "seq", 1) for block in loads[len(steps) :])

    def land(self, loads, gots):
        steps = self.steps()
        self.done += 1
        for (piece, chip), other in zip(self.fresh, gots[len(steps) :]):
            self.pieces += [piece, other]
            self.at += [chip * 2 + self.core, chip * 2 + 1 - self.core]
        self.fresh = []
        for step, got in zip(steps, gots):
            self.moving[step] = got
            self.fresh.append((got, chip_at(self.chips, self.spot - step * self.done)))

    def whole(self):
        while self.fresh:
            slot([self], lambda: ())
        self.place_pieces()
        return self.full.reshape(-1, self.full.shape[-1])


class RingScatter:
    def __init__(self, *grads):
        self.size = lax.axis_size("seq")
        self.chips = self.size // 2
        place = lax.axis_index("seq")
        core, chip = place % 2, place // 2
        self.spot = ring_spot(self.chips, chip)
        self.widths = [grad.shape[1] for grad in grads]
        lows = [grad.astype(jnp.bfloat16).reshape(self.chips, 2, grad.shape[0] // self.size, -1) for grad in grads]

        def side(which):
            parts = [lax.dynamic_index_in_dim(low, which, 1, keepdims=False) for low in lows]
            return jnp.concatenate(parts, axis=-1) if len(parts) > 1 else parts[0]

        self.kept, self.sent = side(core), side(1 - core)
        ahead = self.chips // 2
        self.hops = {1: ahead, -1: self.chips - 1 - ahead}
        self.stage = 0
        self.got = {}
        self.total = None

    def pending(self):
        return self.total is None

    def parts(self):
        ends = [sum(self.widths[:i]) for i in range(len(self.widths) + 1)]
        return tuple(self.total[:, first:last] for first, last in zip(ends, ends[1:]))

    def piece(self, offset):
        at = chip_at(self.chips, self.spot + offset)
        return lax.dynamic_index_in_dim(self.chip_sum, at, 0, keepdims=False).astype(jnp.float32)

    def steps(self):
        return [step for step in (1, -1) if self.stage <= self.hops[step]]

    def load(self):
        if self.stage == 0:
            return (self.sent,)
        if self.steps():
            loads = []
            for step in self.steps():
                moving = self.piece(step * (self.hops[step] - self.stage + 1))
                if self.stage > 1:
                    moving = moving + self.got[step].astype(jnp.float32)
                loads.append(moving.astype(jnp.bfloat16))
            return tuple(loads)
        total = self.piece(0)
        for got in self.got.values():
            total = total + got.astype(jnp.float32)
        return (total.astype(jnp.bfloat16),)

    def fly(self, loads):
        if self.stage == 0:
            return (trade(loads[0], "seq", 1),)
        if self.steps():
            return tuple(
                lax.ppermute(block, "seq", ring_path(self.chips, step)) for block, step in zip(loads, self.steps())
            )
        if lax.axis_size("rows") == 2:
            return (trade(loads[0], "rows", 1),)
        return (lax.psum(loads[0], "rows"),)

    def land(self, loads, gots):
        if self.stage == 0:
            both = self.kept.astype(jnp.float32) + gots[0].astype(jnp.float32)
            self.chip_sum = both.astype(jnp.bfloat16)
        elif self.steps():
            for step, got in zip(self.steps(), gots):
                self.got[step] = got
        else:
            self.total = gots[0].astype(jnp.float32)
            if lax.axis_size("rows") == 2:
                self.total = self.total + loads[0].astype(jnp.float32)
        self.stage += 1


class RowSum:
    def __init__(self, block):
        self.block = block
        self.total = None

    def pending(self):
        return self.total is None

    def load(self):
        return (self.block,)

    def fly(self, loads):
        if lax.axis_size("rows") == 2:
            return (trade(loads[0], "rows", 1),)
        return (lax.psum(loads[0], "rows"),)

    def land(self, loads, gots):
        self.total = gots[0].astype(jnp.float32)
        if lax.axis_size("rows") == 2:
            self.total = self.total + loads[0].astype(jnp.float32)


class AllSum:
    def __init__(self, block):
        self.block = block
        self.rounds = []
        for axis in ("seq", "rows"):
            bit = 1
            while bit < lax.axis_size(axis):
                self.rounds.append((axis, bit))
                bit *= 2

    def pending(self):
        return bool(self.rounds)

    def load(self):
        return (self.block,)

    def fly(self, loads):
        return (trade(loads[0], *self.rounds[0]),)

    def land(self, loads, gots):
        self.block = loads[0] + gots[0]
        self.rounds.pop(0)


class Chain:
    def __init__(self, block, follow):
        self.follow = follow
        self.start(block)

    def start(self, block):
        self.block = block
        self.axis, self.bit = 0, lax.axis_size("seq") // 2

    def pending(self):
        return self.block is not None

    def load(self):
        return (self.block,)

    def fly(self, loads):
        return (trade(loads[0], "seq", self.bit),)

    def land(self, loads, gots):
        upper = (lax.axis_index("seq") & self.bit) > 0
        ends = [jnp.where(upper, gots[0], loads[0]), jnp.where(upper, loads[0], gots[0])]
        self.block = jnp.stack(ends, axis=self.axis)
        self.axis, self.bit = self.axis + 1, self.bit // 2
        if self.bit == 0:
            shape = self.block.shape[self.axis :]
            following = self.follow(self.block.reshape((-1,) + shape[1:]))
            self.block = None
            if following is not None:
                self.start(following)


class ReturnRows:
    def __init__(self, own, borrowed, shards):
        self.own, self.borrowed, self.shards = own, borrowed.astype(jnp.bfloat16), shards
        self.total = None

    def pending(self):
        return self.total is None

    def load(self):
        return (self.borrowed,)

    def fly(self, loads):
        one_sided, turns, sent = row_plan(self.own.shape[1], self.shards)
        if one_sided:
            return (lax.ppermute(loads[0], "rows", [(0, 1), (1, 0)]),)
        gots = []
        for piece, turn in enumerate([-t for t in range(turns, 0, -1)] + list(range(1, turns + 1))):
            block = loads[0][:, piece * sent : (piece + 1) * sent]
            gots.append(lax.ppermute(block, "rows", route(self.shards, turn)))
        return tuple(gots)

    def land(self, loads, gots):
        rows, own = self.own.shape[1], self.own
        one_sided, turns, sent = row_plan(rows, self.shards)
        if one_sided:
            got = gots[0].astype(own.dtype)
            room = [(0, 0)] * own.ndim
            at_end, at_start = list(room), list(room)
            at_end[1], at_start[1] = (rows - sent, 0), (0, rows - sent)
            first = lax.axis_index("rows") == 0
            self.total = own + jnp.where(first, jnp.pad(got, at_end), jnp.pad(got, at_start))
            return
        for piece, got in enumerate(gots):
            span = slice(rows - sent, None) if piece < turns else slice(0, sent)
            own = own.at[:, span].add(got.astype(own.dtype))
        self.total = own


def in_rows(parts):
    flats = [part.reshape(-1) for part in parts]
    return jnp.concatenate([jnp.pad(flat, (0, -flat.size % D)).reshape(-1, D) for flat in flats], axis=0)


def from_rows(rows, parts):
    found, first = [], 0
    for part in parts:
        count = -(-part.size // D)
        found.append(rows[first : first + count].reshape(-1)[: part.size].reshape(part.shape))
        first += count
    return found


def slot(rings, work, *values, wait=()):
    loads = [ring.load() for ring in rings]
    held = lax.optimization_barrier(tuple(values) + sum(loads, ()))
    values, rest = held[: len(values)], held[len(values) :]
    gots = []
    for i, ring in enumerate(rings):
        loads[i], rest = rest[: len(loads[i])], rest[len(loads[i]) :]
        gots.append(ring.fly(loads[i]))
    results = tuple(work(*values))
    held = lax.optimization_barrier(results + tuple(wait) + sum(gots, ()))
    results, rest = held[: len(results)], held[len(results) + len(wait) :]
    for i, ring in enumerate(rings):
        got, rest = rest[: len(gots[i])], rest[len(gots[i]) :]
        ring.land(loads[i], got)
    return results + held[len(results) : len(results) + len(wait)]


def on_device(
    row_shards,
    tokens,
    image_ids,
    timestep,
    norm1_gain,
    norm1_shift,
    time_in_weight,
    time_in_bias,
    time_out_weight,
    time_out_bias,
    mix_weight,
    time_mix_weight,
    position_bias,
    proj_weight,
    proj_bias,
    norm2_gain,
    norm2_shift,
    up_weight,
    up_bias,
    down_weight,
    down_bias,
    cotangent,
):
    seq_rows, local_rows, columns, _ = tokens.shape
    act_tokens = tokens.reshape(seq_rows, local_rows, PACK, GRID, D)
    act_cot = cotangent.reshape(seq_rows, local_rows, PACK, GRID, D)
    token_count = seq_rows * local_rows * columns
    seqs = lax.axis_size("seq")
    place = lax.axis_index("seq")
    images = seqs * seq_rows * PACK
    width_part, freq_part = D // seqs, FREQ // seqs

    def my_part(array, part, axis):
        return lax.dynamic_slice_in_dim(array, place * part, part, axis=axis)

    full_first = lax.all_gather(jnp.concatenate([mix_weight, proj_weight], axis=1), "seq", axis=0, tiled=True)
    full_mix, full_proj = full_first[:, : 3 * D], full_first[:, 3 * D :]
    borrowed, borrowed_at, sent_rows = borrow_rows(act_tokens, row_shards)
    timestep, time_in_weight = lax.optimization_barrier((timestep, time_in_weight, sent_rows))[:2]
    half_width = FREQ // 2
    frequency = jnp.exp(-math.log(10000.0) * jnp.arange(half_width, dtype=jnp.float32) / half_width)

    def time_first(timestep, time_in_weight):
        angles = timestep.astype(jnp.float32).reshape(-1, 1) * frequency
        features = jnp.concatenate([jnp.cos(angles), jnp.sin(angles)], axis=-1).astype(jnp.bfloat16)
        spare = -features.size % D
        features = jnp.pad(features.reshape(-1), (0, spare)).reshape(-1, D)
        both = gather_small(jnp.concatenate([time_in_weight, features], axis=0))
        full_tin = both[:, :freq_part].reshape(FREQ, D)
        features = both[:, freq_part:].reshape(seqs, -1)[:, : seq_rows * PACK * FREQ].reshape(images, FREQ)
        time_pre = jnp.einsum(
            "fd,if->di", my_part(full_tin, width_part, 1), features, preferred_element_type=jnp.float32
        )
        return (features, time_pre + my_part(time_in_bias, width_part, 0)[:, None])

    def time_second(time_pre):
        time_hidden = jax.nn.silu(time_pre).astype(jnp.bfloat16)
        partial = jnp.einsum("fd,fi->di", time_out_weight, time_hidden, preferred_element_type=jnp.float32)
        time_embed = scatter_small(partial.reshape(seqs, width_part, images))
        time_embed = time_embed + my_part(time_out_bias, width_part, 0)[:, None]
        return (time_hidden, time_embed.astype(jnp.bfloat16))

    def time_third(time_embed):
        partial = jnp.einsum("di,de->ie", time_embed, time_mix_weight, preferred_element_type=jnp.float32)
        return (scatter_small(partial.reshape(seqs, seq_rows * PACK, 3 * D)),)

    features, time_pre = time_first(timestep, time_in_weight)
    time_hidden, time_embed = time_second(time_pre)
    key_at = jnp.concatenate([jnp.arange(local_rows), borrowed_at])
    key_row = lax.axis_index("rows") * local_rows + key_at
    key_rows = jnp.where((key_row >= 0) & (key_row < GRID), key_at, 4 * GRID).astype(jnp.int32)
    table = bias_table(position_bias, key_rows, local_rows)
    time_embed = after(time_embed, table)
    (time_proj,) = time_third(time_embed)
    time_proj = time_proj.reshape(seq_rows, PACK, 3 * D)
    my_features = my_part(features, freq_part, 1)
    block_slots = image_ids[:, ::GRID]
    slot_hot = (block_slots[:, :, None] == jnp.arange(PACK, dtype=jnp.int32)[None, None, :]).astype(
        jnp.float32
    )
    unit_time = jnp.einsum("skp,spe->ske", slot_hot, time_proj, precision=highest)
    ext_tokens = jnp.concatenate([act_tokens, borrowed], axis=1)
    ext_rows = ext_tokens.shape[1]
    ext_count = seq_rows * ext_rows * columns

    normed1 = norm_forward(ext_tokens.astype(jnp.float32), norm1_gain, norm1_shift)[0].astype(jnp.bfloat16)
    full_up = lax.all_gather(up_weight, "seq", axis=0, tiled=True)
    down_ring = RingGather(after(down_weight, full_first[:8, :128]))

    def to_mixed(normed1):
        return ((low_dot(normed1, full_mix) + unit_time[:, None, :, None, :]).astype(jnp.bfloat16),)

    (mixed,) = slot([down_ring], to_mixed, normed1)
    (attended,) = slot([down_ring], lambda mixed: (attend(mixed, table, local_rows),), mixed)
    flat_tokens = act_tokens.astype(jnp.float32)

    def second_norm(attended):
        residual = flat_tokens + low_dot(attended, full_proj) + proj_bias
        normed2, unit_two, inverse_two = norm_forward(residual, norm2_gain, norm2_shift)
        return (residual, normed2.astype(jnp.bfloat16), unit_two, inverse_two)

    down_ring.place_pieces()
    attended = after(attended, down_ring.full)
    residual, normed2, unit_two, inverse_two = slot([down_ring], second_norm, attended)

    def to_hidden(normed2):
        pre = low_dot(normed2, full_up) + up_bias
        slope = math.sqrt(2.0 / math.pi)
        square = pre * pre
        bend = jnp.tanh(slope * pre * (1.0 + 0.044715 * square))
        half = 0.5 * (1.0 + bend)
        gelu_slope = half + 0.5 * pre * (1.0 - bend * bend) * (slope * (1.0 + 3.0 * 0.044715 * square))
        return ((pre * half).astype(jnp.bfloat16), gelu_slope.astype(jnp.bfloat16))

    hidden, gelu_slope = slot([down_ring], to_hidden, normed2)
    flat_hidden = hidden.reshape(token_count, FF)
    flat_cot = act_cot.reshape(token_count, D)

    def weight_down(flat_hidden):
        grad = jnp.einsum("nf,nd->fd", flat_hidden, flat_cot, preferred_element_type=jnp.float32)
        return (grad.astype(jnp.bfloat16),)

    (grad_down_w,) = slot([down_ring], weight_down, flat_hidden)
    full_down = down_ring.whole()
    grad_down_b = jnp.sum(flat_cot, axis=0, dtype=jnp.float32)
    down_part = lax.psum_scatter(grad_down_w, "seq", scatter_dimension=0, tiled=True)
    grad_hidden = jnp.einsum(
        "nd,fd->nf", flat_cot, full_down, preferred_element_type=jnp.float32
    )
    grad_pre = (grad_hidden * gelu_slope.reshape(token_count, FF).astype(jnp.float32)).astype(jnp.bfloat16)
    flat_normed2 = normed2.reshape(token_count, D)
    grad_up_w = jnp.einsum("nd,nf->df", flat_normed2, grad_pre, preferred_element_type=jnp.float32)
    grad_up_b = jnp.sum(grad_pre, axis=0, dtype=jnp.float32)
    def back_up(grad_pre):
        grad_normed2 = jnp.einsum("nf,df->nd", grad_pre, full_up, preferred_element_type=jnp.float32)
        return (grad_normed2.reshape(act_tokens.shape),)

    def back_norm(grad_normed2):
        grad_norm_two, grad_gain_two, grad_shift_two = norm_backward(
            grad_normed2, unit_two, inverse_two, norm2_gain
        )
        grad_residual = act_cot.astype(jnp.float32) + grad_norm_two
        grad_branch = grad_residual.astype(jnp.bfloat16).reshape(token_count, D)
        grad_proj_w = jnp.einsum(
            "nd,ne->de", attended.reshape(token_count, D), grad_branch, preferred_element_type=jnp.float32
        ).astype(jnp.bfloat16)
        grad_proj_b = jnp.sum(grad_branch, axis=0, dtype=jnp.float32)
        grad_attended = jnp.einsum(
            "ne,de->nd", grad_branch, full_proj, preferred_element_type=jnp.float32
        ).astype(jnp.bfloat16)
        grad_attended = grad_attended.reshape(act_tokens.shape)
        return (grad_residual, grad_gain_two, grad_shift_two, grad_proj_w, grad_proj_b, grad_attended)

    grad_up_w = grad_up_w.astype(jnp.bfloat16)
    (grad_normed2,) = back_up(grad_pre)
    up_sum = RingScatter(grad_up_w)
    (grad_residual, grad_gain_two, grad_shift_two, grad_proj_w, grad_proj_b, grad_attended) = slot(
        [up_sum], back_norm, grad_normed2
    )
    proj_part = lax.psum_scatter(grad_proj_w, "seq", scatter_dimension=0, tiled=True)
    part = -(-seq_rows // 2)
    spans = [slice(0, part), slice(part, seq_rows)][: min(2, seq_rows)]
    grad_mixed, grad_tables, grad_units = None, [], []
    for span in spans:
        held = (grad_attended,) if grad_mixed is None else (grad_attended, grad_mixed)
        grad_mixed, grad_table, grad_unit = slot(
            [up_sum], lambda grad, kept=None: attend_back(mixed, grad, table, kept, span, local_rows), *held
        )
        grad_tables.append(grad_table)
        grad_units.append(grad_unit)
    grad_unit = jnp.concatenate(grad_units, axis=0)
    unit_sum, down_sum = RowSum(grad_unit), RowSum(down_part)

    def weight_mix(grad_mixed):
        grad_mix_w = jnp.einsum(
            "nd,ne->de",
            normed1.reshape(ext_count, D),
            grad_mixed.reshape(ext_count, 3 * D),
            preferred_element_type=jnp.float32,
        )
        return (grad_mix_w.astype(jnp.bfloat16),)

    (grad_mix_w,) = slot([unit_sum, up_sum, down_sum], weight_mix, grad_mixed)
    found = {}

    def from_time_proj(gathered):
        found["tmix"] = low_dot(time_embed, gathered)
        grad_embed = jnp.einsum("de,ie->di", time_mix_weight, gathered, preferred_element_type=jnp.float32)
        chain.follow = from_embed
        return grad_embed.astype(jnp.bfloat16)

    def from_embed(gathered):
        found["tout"] = jnp.einsum("fi,di->fd", time_hidden, gathered, preferred_element_type=jnp.float32)
        found["tout_b"] = jnp.sum(gathered, axis=1, dtype=jnp.float32)
        silu_back = jax.vjp(jax.nn.silu, time_pre)[1]
        chain.follow = from_pre
        return silu_back(low_dot(time_out_weight, gathered))[0].astype(jnp.bfloat16)

    def from_pre(gathered):
        found["tin"] = jnp.einsum("if,di->fd", my_features, gathered, preferred_element_type=jnp.float32)
        found["tin_b"] = jnp.sum(gathered, axis=1, dtype=jnp.float32)

    grad_time_proj = jnp.einsum("skp,ske->spe", slot_hot, unit_sum.total, precision=highest)
    chain = Chain(grad_time_proj.astype(jnp.bfloat16).reshape(-1, 3 * D), from_time_proj)
    mix_part = lax.psum_scatter(grad_mix_w, "seq", scatter_dimension=0, tiled=True)
    first_sums = (grad_proj_b, grad_gain_two, grad_shift_two, grad_up_b, grad_down_b)
    rings = [up_sum, chain]

    def run(work, *values):
        return slot([ring for ring in rings if ring.pending()], work, *values)

    def back_mixed(grad_mixed, span):
        rows = grad_mixed[span]
        grad_in = jnp.einsum("spcge,de->spcgd", rows, full_mix, preferred_element_type=jnp.float32)
        return (grad_in[:, :local_rows], grad_in[:, local_rows:].astype(jnp.bfloat16))

    def back_first(grad_normed1, tokens, grad_residual, span):
        _, unit_one, inverse_one = norm_forward(tokens[span].astype(jnp.float32), norm1_gain, norm1_shift)
        grad_norm_one, gain, shift = norm_backward(grad_normed1, unit_one, inverse_one, norm1_gain)
        return ((grad_residual[span] + grad_norm_one).astype(jnp.bfloat16), gain, shift)

    def last_part(hidden, residual, span):
        return ((residual[span] + low_dot(hidden[span], full_down) + down_bias).astype(jnp.bfloat16),)

    (bias_grad,) = run(lambda *pairs: (bias_sum(pairs, key_rows, local_rows),), *grad_tables)
    returned = []
    for span in spans:
        returned.append(ReturnRows(*run(functools.partial(back_mixed, span=span), grad_mixed), row_shards))
        rings.append(returned[-1])
    outputs, tokens_grads, firsts = [], [], []

    def finish(span):
        outputs.extend(run(functools.partial(last_part, span=span), hidden, residual))

    finish(spans[0])
    for span, back in zip(spans, returned):
        firsts.append(run(functools.partial(back_first, span=span), back.total, act_tokens, grad_residual))
        tokens_grads.append(firsts[-1][0])
    grad_gain_one, grad_shift_one = (sum(part) for part in zip(*[first[1:] for first in firsts]))
    late_sums = (grad_gain_one, grad_shift_one, bias_grad) + first_sums
    late_sum = AllSum(in_rows(late_sums))
    proj_sum, mix_sum = RowSum(proj_part), RowSum(mix_part)
    rings += [late_sum, proj_sum]
    for span in spans[1:]:
        finish(span)
    output = jnp.concatenate(outputs, axis=0)
    tokens_grad = jnp.concatenate(tokens_grads, axis=0)
    while any(ring.pending() for ring in rings):
        run(lambda: ())
    slot([mix_sum], lambda: ())

    (gain_one, shift_one, bias_total, proj_total, gain_two, shift_two, up_total, down_total) = from_rows(
        late_sum.block, late_sums
    )
    sum_down, sum_up, sum_mix, sum_proj = down_sum.total, up_sum.total, mix_sum.total, proj_sum.total
    sum_tmix, sum_tout, sum_tin = found["tmix"], found["tout"], found["tin"]
    tout_bias, tin_bias = found["tout_b"], found["tin_b"]
    output = output.reshape(tokens.shape)
    tokens_grad = tokens_grad.reshape(tokens.shape)
    return (
        output,
        tokens_grad,
        gain_one,
        shift_one,
        sum_tin,
        tin_bias,
        sum_tout,
        tout_bias,
        sum_mix,
        sum_tmix,
        bias_total,
        sum_proj,
        proj_total,
        gain_two,
        shift_two,
        sum_up,
        up_total,
        sum_down,
        down_total,
    )


def solution(mesh):
    whole, sharded = (P(), P("seq", None))
    acts = P("seq", "rows", None, None)
    return jax.shard_map(
        functools.partial(on_device, mesh.shape["rows"]),
        mesh=mesh,
        in_specs=(
            acts,
            sharded,
            sharded,
            whole,
            whole,
            sharded,
            whole,
            sharded,
            whole,
            sharded,
            sharded,
            whole,
            sharded,
            whole,
            whole,
            whole,
            sharded,
            whole,
            sharded,
            whole,
            acts,
        ),
        out_specs=(
            acts,
            acts,
            whole,
            whole,
            sharded,
            whole,
            sharded,
            whole,
            sharded,
            sharded,
            whole,
            sharded,
            whole,
            whole,
            whole,
            sharded,
            whole,
            sharded,
            whole,
        ),
        check_vma=False,
    )
```

```python
import functools
import math

import jax
import jax.numpy as jnp
from jax import lax
from jax.experimental import pallas as pl
from jax.experimental.pallas import tpu as pltpu
from jax.sharding import PartitionSpec as P

D = 1152
HEADS = 16
HEAD_DIM = 72
FF = 4608
FREQ = 256
GRID = 16
PACK = 4
REACH = 4
LANES = 128


epsilon = 1e-06
floor_score = -1e30
highest = lax.Precision.HIGHEST
score_scale = HEAD_DIM ** (-0.5)


def low_dot(left, right):
    return jnp.dot(left, right, preferred_element_type=jnp.float32)


def norm_forward(values, norm_gain, norm_shift):
    centred = values - jnp.mean(values, axis=-1, keepdims=True)
    inverse = lax.rsqrt(jnp.mean(centred * centred, axis=-1, keepdims=True) + epsilon)
    unit_rows = centred * inverse
    return (unit_rows * norm_gain + norm_shift, unit_rows, inverse)


def norm_backward(grad_out, unit_rows, inverse, norm_gain):
    scaled = grad_out * norm_gain
    grad_in = inverse * (
        scaled
        - jnp.mean(scaled, axis=-1, keepdims=True)
        - unit_rows * jnp.mean(scaled * unit_rows, axis=-1, keepdims=True)
    )
    leading = tuple(range(grad_out.ndim - 1))
    return (grad_in, jnp.sum(grad_out * unit_rows, axis=leading), jnp.sum(grad_out, axis=leading))


def row_plan(local_rows, shards):
    if shards == 2 and local_rows >= REACH:
        return (True, 1, REACH)
    sent = min(local_rows, REACH)
    return (False, -(-REACH // local_rows), sent)


def route(shards, distance):
    return [(i - distance, i) for i in range(shards) if 0 <= i - distance < shards]


def borrow_rows(own, shards):
    rows = own.shape[1]
    one_sided, turns, sent = row_plan(rows, shards)
    place = lax.axis_index("rows")
    if one_sided:
        start = jnp.where(place == 0, rows - sent, 0)
        block = lax.dynamic_slice_in_dim(own, start, sent, axis=1)
        got = lax.ppermute(block, "rows", [(0, 1), (1, 0)])
        first = jnp.where(place == 0, rows, -sent)
        return (got, first + jnp.arange(sent), block)
    pieces, where = [], []
    for turn in range(turns, 0, -1):
        pieces.append(lax.ppermute(own[:, rows - sent :], "rows", route(shards, turn)))
        where.append(jnp.arange(sent) - (turn - 1) * rows - sent)
    for turn in range(1, turns + 1):
        pieces.append(lax.ppermute(own[:, :sent], "rows", route(shards, -turn)))
        where.append(jnp.arange(sent) + turn * rows)
    return (jnp.concatenate(pieces, axis=1), jnp.concatenate(where), own[:, :sent])


def head_window(head):
    first, last = head * HEAD_DIM, (head + 1) * HEAD_DIM
    return (first // LANES * LANES, -(-last // LANES) * LANES)


def head_mask(head, dtype):
    low, high = head_window(head)
    lane = lax.broadcasted_iota(jnp.int32, (1, high - low), 1) + low
    return ((lane >= head * HEAD_DIM) & (lane < (head + 1) * HEAD_DIM)).astype(dtype)


def nt_dot(left, right):
    return lax.dot_general(left, right, (((1,), (1,)), ((), ())), preferred_element_type=jnp.float32)


def tn_dot(left, right):
    return lax.dot_general(left, right, (((0,), (0,)), ((), ())), preferred_element_type=jnp.float32)


def table_kernel(bias_ref, row_ref, out_ref, *, own, rows):
    head = pl.program_id(0)
    reach = 2 * REACH + 1
    lane = lax.broadcasted_iota(jnp.int32, (GRID, own), 1)
    query_row, query_col = lane // GRID, lane % GRID
    col_diff = lax.broadcasted_iota(jnp.int32, (GRID, own), 0) - query_col
    floor = jnp.full((GRID, own), floor_score, jnp.float32)
    by_row = []
    for n in range(reach):
        value = floor
        for o in range(reach):
            value = jnp.where(col_diff == o - REACH, bias_ref[head, n * reach + o], value)
        by_row.append(value)
    for b in range(rows):
        row_diff = row_ref[b] - query_row
        value = floor
        for n in range(reach):
            value = jnp.where(row_diff == n - REACH, by_row[n], value)
        out_ref[0, b * GRID : (b + 1) * GRID, :] = value


def bias_table(position_bias, key_rows, own_rows):
    rows = key_rows.shape[0]
    own, total = own_rows * GRID, rows * GRID
    smem = pl.BlockSpec(memory_space=pltpu.SMEM)
    return pl.pallas_call(
        functools.partial(table_kernel, own=own, rows=rows),
        grid=(HEADS,),
        in_specs=[smem, smem],
        out_specs=pl.BlockSpec((1, total, own), lambda h: (h, 0, 0)),
        out_shape=jax.ShapeDtypeStruct((HEADS, total, own), jnp.float32),
        name="bias_table",
    )(position_bias.reshape(HEADS, -1), key_rows)


def assemble_kernel(at_ref, *refs, count):
    pieces, out_ref, room, into, out_of = refs[:count], refs[-4], refs[-3], refs[-2], refs[-1]
    first = [pltpu.make_async_copy(piece, room.at[i], into.at[i]) for i, piece in enumerate(pieces)]
    second = [pltpu.make_async_copy(room.at[i], out_ref.at[at_ref[i]], out_of.at[i]) for i in range(len(pieces))]
    for copy in first:
        copy.start()
    for one, two in zip(first, second):
        one.wait()
        two.start()
    for copy in second:
        copy.wait()


def assemble(pieces, at, size, kept=None):
    anywhere = pl.BlockSpec(memory_space=pl.ANY)
    shape, dtype, count = pieces[0].shape, pieces[0].dtype, len(pieces)
    return pl.pallas_call(
        functools.partial(assemble_kernel, count=len(pieces)),
        grid_spec=pltpu.PrefetchScalarGridSpec(
            num_scalar_prefetch=1,
            grid=(1,),
            in_specs=[anywhere] * (count if kept is None else count + 1),
            out_specs=anywhere,
            scratch_shapes=[
                pltpu.VMEM((count,) + shape, dtype),
                pltpu.SemaphoreType.DMA((count,)),
                pltpu.SemaphoreType.DMA((count,)),
            ],
        ),
        out_shape=jax.ShapeDtypeStruct((size,) + shape, dtype),
        input_output_aliases={} if kept is None else {count + 1: 0},
        compiler_params=pltpu.CompilerParams(vmem_limit_bytes=48 << 20),
        name="assemble",
    )(at, *pieces, *(() if kept is None else (kept,)))


def bias_sum_kernel(*refs, own, rows):
    pair_refs, row_ref, out_ref = refs[:-2], refs[-2], refs[-1]
    reach = 2 * REACH + 1
    lane = lax.broadcasted_iota(jnp.int32, (GRID, own), 1)
    query_row, query_col = lane // GRID, lane % GRID
    col_diff = lax.broadcasted_iota(jnp.int32, (GRID, own), 0) - query_col
    zero = jnp.zeros((GRID, own), jnp.float32)
    for head in range(out_ref.shape[0]):
        by_row = [zero] * reach
        for b in range(rows):
            block = sum(pairs[head, b * GRID : (b + 1) * GRID, :] for pairs in pair_refs)
            row_diff = row_ref[b] - query_row
            for n in range(reach):
                by_row[n] = by_row[n] + jnp.where(row_diff == n - REACH, block, zero)
        for n in range(reach):
            for o in range(reach):
                kept = jnp.where(col_diff == o - REACH, by_row[n], zero)
                out_ref[head, n * reach + o, :] = jnp.sum(kept, axis=0)


def bias_sum(pairs, key_rows, own_rows):
    reach = 2 * REACH + 1
    rows = key_rows.shape[0]
    own, total = own_rows * GRID, rows * GRID
    heads = 4
    block = pl.BlockSpec((heads, total, own), lambda h: (h, 0, 0))
    by_lane = pl.pallas_call(
        functools.partial(bias_sum_kernel, own=own, rows=rows),
        grid=(HEADS // heads,),
        in_specs=[block] * len(pairs) + [pl.BlockSpec(memory_space=pltpu.SMEM)],
        out_specs=pl.BlockSpec((heads, reach * reach, own), lambda h: (h, 0, 0)),
        out_shape=jax.ShapeDtypeStruct((HEADS, reach * reach, own), jnp.float32),
        name="bias_sum",
    )(*pairs, key_rows)
    return jnp.sum(by_lane, axis=-1).reshape(HEADS, reach, reach)


def attend_kernel(mixed_ref, table_ref, out_ref, acc_ref, *, own, total):
    def columns(part, low, high, count):
        block = mixed_ref[0, : count // GRID, 0, :, part * D + low : part * D + high]
        return block.reshape(count, high - low)

    for head in range(HEADS):
        low, high = head_window(head)
        query = columns(0, low, high, own) * head_mask(head, jnp.bfloat16)
        scores = nt_dot(columns(1, low, high, total), query) * score_scale + table_ref[head]
        top = jnp.max(scores, axis=0, keepdims=True)
        weight = jnp.exp(scores - top)
        weight = weight * (1.0 / jnp.sum(weight, axis=0, keepdims=True))
        result = tn_dot(weight.astype(jnp.bfloat16), columns(2, low, high, total))
        if head * HEAD_DIM % LANES == 0:
            acc_ref[:, low:high] = result
        else:
            mine = head_mask(head, jnp.float32)
            earlier = acc_ref[:, low : low + LANES]
            acc_ref[:, low : low + LANES] = jnp.where(mine[:, :LANES] > 0, result[:, :LANES], earlier)
            if high - low > LANES:
                acc_ref[:, low + LANES : high] = result[:, LANES:]
    out_ref[0, :, 0] = acc_ref[...].astype(jnp.bfloat16).reshape(own // GRID, GRID, D)


def attend_back_kernel(mixed_ref, grad_ref, table_ref, *refs, own, total):
    out_ref, bias_ref, unit_ref, q_ref, k_ref, v_ref = refs[-6:]

    @pl.when((pl.program_id(0) == 0) & (pl.program_id(1) == 0))
    def _():
        bias_ref[...] = jnp.zeros_like(bias_ref)

    def columns(part, low, high, count):
        block = mixed_ref[0, : count // GRID, 0, :, part * D + low : part * D + high]
        return block.reshape(count, high - low)

    def put(ref, low, high, value, fresh):
        if fresh:
            ref[:, low:high] = value
        else:
            ref[:, low : low + LANES] += value[:, :LANES]
            if high - low > LANES:
                ref[:, low + LANES : high] = value[:, LANES:]

    for head in range(HEADS):
        low, high = head_window(head)
        fresh = head * HEAD_DIM % LANES == 0
        keep = head_mask(head, jnp.bfloat16)
        query = columns(0, low, high, own) * keep
        grad = grad_ref[0, :, 0, :, low:high].reshape(own, high - low) * keep
        keys = columns(1, low, high, total)
        scores = nt_dot(keys, query) * score_scale + table_ref[head]
        top = jnp.max(scores, axis=0, keepdims=True)
        weight = jnp.exp(scores - top)
        weight = weight * (1.0 / jnp.sum(weight, axis=0, keepdims=True))
        grad_weight = nt_dot(columns(2, low, high, total), grad)
        delta = jnp.sum(weight * grad_weight, axis=0, keepdims=True)
        grad_scores = weight * (grad_weight - delta)
        bias_ref[head] += grad_scores
        grad_low = grad_scores.astype(jnp.bfloat16)
        put(v_ref, low, high, low_dot(weight.astype(jnp.bfloat16), grad), fresh)
        put(k_ref, low, high, low_dot(grad_low, query), fresh)
        put(q_ref, low, high, tn_dot(grad_low, keys) * head_mask(head, jnp.float32), fresh)
    rows, own_rows = total // GRID, own // GRID
    out_ref[0, :own_rows, 0, :, :D] = (q_ref[...] * score_scale).astype(jnp.bfloat16).reshape(own_rows, GRID, D)
    if rows > own_rows:
        out_ref[0, own_rows:, 0, :, :D] = jnp.zeros((rows - own_rows, GRID, D), jnp.bfloat16)
    out_ref[0, :, 0, :, D : 2 * D] = (k_ref[...] * score_scale).astype(jnp.bfloat16).reshape(rows, GRID, D)
    out_ref[0, :, 0, :, 2 * D :] = v_ref[...].astype(jnp.bfloat16).reshape(rows, GRID, D)
    slot_at = pl.program_id(1)
    for part, ref, scale in ((0, q_ref, score_scale), (1, k_ref, score_scale), (2, v_ref, 1.0)):
        low = (ref[...] * scale).astype(jnp.bfloat16).astype(jnp.float32)
        unit_ref[0, pl.ds(slot_at, 1), part * D : (part + 1) * D] = jnp.sum(low, axis=0, keepdims=True)


def attend(mixed, table, own_rows):
    seqs, rows = mixed.shape[:2]
    own, total = own_rows * GRID, rows * GRID
    return pl.pallas_call(
        functools.partial(attend_kernel, own=own, total=total),
        grid=(seqs, PACK),
        in_specs=[
            pl.BlockSpec((1, rows, 1, GRID, 3 * D), lambda s, p: (s, 0, p, 0, 0)),
            pl.BlockSpec((HEADS, total, own), lambda s, p: (0, 0, 0)),
        ],
        out_specs=pl.BlockSpec((1, own_rows, 1, GRID, D), lambda s, p: (s, 0, p, 0, 0)),
        out_shape=jax.ShapeDtypeStruct((seqs, own_rows, PACK, GRID, D), jnp.bfloat16),
        scratch_shapes=[pltpu.VMEM((own, D), jnp.float32)],
        compiler_params=pltpu.CompilerParams(
            dimension_semantics=("arbitrary", "arbitrary"), vmem_limit_bytes=48 << 20
        ),
        name="attend",
    )(mixed, table)


def attend_back(mixed, grad, table, kept, span, own_rows):
    seqs, rows = mixed.shape[:2]
    own, total = own_rows * GRID, rows * GRID
    first = span.start
    kept = () if kept is None else (kept,)
    return pl.pallas_call(
        functools.partial(attend_back_kernel, own=own, total=total),
        grid=(span.stop - span.start, PACK),
        in_specs=[
            pl.BlockSpec((1, rows, 1, GRID, 3 * D), lambda s, p: (first + s, 0, p, 0, 0)),
            pl.BlockSpec((1, own_rows, 1, GRID, D), lambda s, p: (first + s, 0, p, 0, 0)),
            pl.BlockSpec((HEADS, total, own), lambda s, p: (0, 0, 0)),
        ]
        + [pl.BlockSpec(memory_space=pl.ANY)] * len(kept),
        out_specs=[
            pl.BlockSpec((1, rows, 1, GRID, 3 * D), lambda s, p: (first + s, 0, p, 0, 0)),
            pl.BlockSpec((HEADS, total, own), lambda s, p: (0, 0, 0)),
            pl.BlockSpec((1, PACK, 3 * D), lambda s, p: (s, 0, 0)),
        ],
        out_shape=[
            jax.ShapeDtypeStruct((seqs, rows, PACK, GRID, 3 * D), jnp.bfloat16),
            jax.ShapeDtypeStruct((HEADS, total, own), jnp.float32),
            jax.ShapeDtypeStruct((span.stop - span.start, PACK, 3 * D), jnp.float32),
        ],
        scratch_shapes=[
            pltpu.VMEM((own, D), jnp.float32),
            pltpu.VMEM((total, D), jnp.float32),
            pltpu.VMEM((total, D), jnp.float32),
        ],
        input_output_aliases={3: 0} if kept else {},
        compiler_params=pltpu.CompilerParams(
            dimension_semantics=("arbitrary", "arbitrary"), vmem_limit_bytes=48 << 20
        ),
        name="attend_back",
    )(mixed, grad, table, *kept)


def trade(block, axis, bit):
    size = lax.axis_size(axis)
    return lax.ppermute(block, axis, [(i, i ^ bit) for i in range(size)])


def gather_small(block):
    size = lax.axis_size("seq")
    place = lax.axis_index("seq")
    axis, bit = 0, size // 2
    while bit:
        got = trade(block, "seq", bit)
        upper = (place & bit) > 0
        block = jnp.stack([jnp.where(upper, got, block), jnp.where(upper, block, got)], axis=axis)
        axis, bit = axis + 1, bit // 2
    return block.reshape((size,) + block.shape[axis:])


def scatter_small(block, sent_as=jnp.float32):
    size = lax.axis_size("seq")
    place = lax.axis_index("seq")
    bit = 1
    while bit < size:
        block = block.reshape((block.shape[0] // 2, 2) + block.shape[1:])
        upper = (place & bit) > 0
        kept = jnp.where(upper, block[:, 1], block[:, 0])
        sent = jnp.where(upper, block[:, 0], block[:, 1])
        block = kept + trade(sent.astype(sent_as), "seq", bit).astype(jnp.float32)
        bit *= 2
    return block[0]


def after(value, *earlier):
    return lax.optimization_barrier((value,) + earlier)[0]


def ring_order(chips):
    return list(range(0, chips, 2)) + list(range(1, chips, 2))[::-1]


def ring_path(chips, step):
    order = ring_order(chips)
    return [(2 * order[i] + c, 2 * order[(i + step) % chips] + c) for i in range(chips) for c in range(2)]


def ring_spot(chips, chip):
    return jnp.where(chip % 2 == 0, chip // 2, chips - 1 - chip // 2)


def chip_at(chips, spot):
    spot = (spot + chips) % chips
    return jnp.where(spot < chips // 2, 2 * spot, 2 * chips - 1 - 2 * spot)


class RingGather:
    def __init__(self, shard):
        self.size = lax.axis_size("seq")
        self.chips = self.size // 2
        place = lax.axis_index("seq")
        self.core, self.chip = place % 2, place // 2
        self.spot = ring_spot(self.chips, self.chip)
        ahead = self.chips // 2
        self.hops = {1: ahead, -1: self.chips - 1 - ahead}
        self.moving = {1: shard, -1: shard}
        self.done = 0
        self.fresh = [(shard, self.chip)]
        self.pieces, self.at = [], []
        self.full = None

    def place_pieces(self):
        self.full = assemble(self.pieces, jnp.stack(self.at).astype(jnp.int32), self.size, self.full)
        self.pieces, self.at = [], []

    def steps(self):
        return [step for step in (1, -1) if self.done < self.hops[step]]

    def load(self):
        return tuple(self.moving[step] for step in self.steps()) + tuple(piece for piece, _ in self.fresh)

    def fly(self, loads):
        steps = self.steps()
        gots = tuple(
            lax.ppermute(block, "seq", ring_path(self.chips, step)) for block, step in zip(loads, steps)
        )
        return gots + tuple(trade(block, "seq", 1) for block in loads[len(steps) :])

    def land(self, loads, gots):
        steps = self.steps()
        self.done += 1
        for (piece, chip), other in zip(self.fresh, gots[len(steps) :]):
            self.pieces += [piece, other]
            self.at += [chip * 2 + self.core, chip * 2 + 1 - self.core]
        self.fresh = []
        for step, got in zip(steps, gots):
            self.moving[step] = got
            self.fresh.append((got, chip_at(self.chips, self.spot - step * self.done)))

    def whole(self):
        while self.fresh:
            slot([self], lambda: ())
        self.place_pieces()
        return self.full.reshape(-1, self.full.shape[-1])


class RingScatter:
    def __init__(self, *grads):
        self.size = lax.axis_size("seq")
        self.chips = self.size // 2
        place = lax.axis_index("seq")
        core, chip = place % 2, place // 2
        self.spot = ring_spot(self.chips, chip)
        self.widths = [grad.shape[1] for grad in grads]
        lows = [grad.astype(jnp.bfloat16).reshape(self.chips, 2, grad.shape[0] // self.size, -1) for grad in grads]

        def side(which):
            parts = [lax.dynamic_index_in_dim(low, which, 1, keepdims=False) for low in lows]
            return jnp.concatenate(parts, axis=-1) if len(parts) > 1 else parts[0]

        self.kept, self.sent = side(core), side(1 - core)
        ahead = self.chips // 2
        self.hops = {1: ahead, -1: self.chips - 1 - ahead}
        self.stage = 0
        self.got = {}
        self.total = None

    def pending(self):
        return self.total is None

    def parts(self):
        ends = [sum(self.widths[:i]) for i in range(len(self.widths) + 1)]
        return tuple(self.total[:, first:last] for first, last in zip(ends, ends[1:]))

    def piece(self, offset):
        at = chip_at(self.chips, self.spot + offset)
        return lax.dynamic_index_in_dim(self.chip_sum, at, 0, keepdims=False).astype(jnp.float32)

    def steps(self):
        return [step for step in (1, -1) if self.stage <= self.hops[step]]

    def load(self):
        if self.stage == 0:
            return (self.sent,)
        if self.steps():
            loads = []
            for step in self.steps():
                moving = self.piece(step * (self.hops[step] - self.stage + 1))
                if self.stage > 1:
                    moving = moving + self.got[step].astype(jnp.float32)
                loads.append(moving.astype(jnp.bfloat16))
            return tuple(loads)
        total = self.piece(0)
        for got in self.got.values():
            total = total + got.astype(jnp.float32)
        return (total.astype(jnp.bfloat16),)

    def fly(self, loads):
        if self.stage == 0:
            return (trade(loads[0], "seq", 1),)
        if self.steps():
            return tuple(
                lax.ppermute(block, "seq", ring_path(self.chips, step)) for block, step in zip(loads, self.steps())
            )
        if lax.axis_size("rows") == 2:
            return (trade(loads[0], "rows", 1),)
        return (lax.psum(loads[0], "rows"),)

    def land(self, loads, gots):
        if self.stage == 0:
            both = self.kept.astype(jnp.float32) + gots[0].astype(jnp.float32)
            self.chip_sum = both.astype(jnp.bfloat16)
        elif self.steps():
            for step, got in zip(self.steps(), gots):
                self.got[step] = got
        else:
            self.total = gots[0].astype(jnp.float32)
            if lax.axis_size("rows") == 2:
                self.total = self.total + loads[0].astype(jnp.float32)
        self.stage += 1


class RowSum:
    def __init__(self, block):
        self.block = block
        self.total = None

    def pending(self):
        return self.total is None

    def load(self):
        return (self.block,)

    def fly(self, loads):
        if lax.axis_size("rows") == 2:
            return (trade(loads[0], "rows", 1),)
        return (lax.psum(loads[0], "rows"),)

    def land(self, loads, gots):
        self.total = gots[0].astype(jnp.float32)
        if lax.axis_size("rows") == 2:
            self.total = self.total + loads[0].astype(jnp.float32)


class AllSum:
    def __init__(self, block):
        self.block = block
        self.rounds = [("seq", [1])]
        bit, rows = 2, 1
        while bit < lax.axis_size("seq"):
            pair = bit * 2 < lax.axis_size("seq")
            self.rounds.append(("seq", [bit, 2 * bit, 3 * bit] if pair else [bit]))
            bit *= 4 if pair else 2
        while rows < lax.axis_size("rows"):
            self.rounds.append(("rows", [rows]))
            rows *= 2

    def pending(self):
        return bool(self.rounds)

    def load(self):
        return (self.block,)

    def fly(self, loads):
        axis, partners = self.rounds[0]
        return tuple(trade(loads[0], axis, partner) for partner in partners)

    def land(self, loads, gots):
        self.block = loads[0] + gots[0]
        if len(gots) == 3:
            self.block = self.block + (gots[1] + gots[2])
        self.rounds.pop(0)


class Chain:
    def __init__(self, block, follow):
        self.follow = follow
        self.start(block)

    def start(self, block):
        self.block = block
        self.axis, self.bit = 0, lax.axis_size("seq") // 2

    def pending(self):
        return self.block is not None

    def load(self):
        return (self.block,)

    def partners(self):
        return [self.bit // 2, self.bit, self.bit + self.bit // 2] if self.bit > 2 else [self.bit]

    def fly(self, loads):
        return tuple(trade(loads[0], "seq", partner) for partner in self.partners())

    def land(self, loads, gots):
        bits = [self.bit, self.bit // 2] if len(gots) == 3 else [self.bit]
        place = lax.axis_index("seq")
        blocks = list(loads + gots)
        for flip, bit in enumerate(bits[::-1]):
            upper = (place & bit) > 0
            blocks = [
                jnp.where(upper, blocks[i ^ (1 << flip)], blocks[i]) for i in range(len(blocks))
            ]
        if len(bits) == 2:
            blocks = [jnp.stack(blocks[:2], axis=self.axis), jnp.stack(blocks[2:], axis=self.axis)]
        self.block = jnp.stack(blocks, axis=self.axis)
        self.axis += len(bits)
        self.bit = bits[-1] // 2
        if self.bit == 0:
            shape = self.block.shape[self.axis :]
            following = self.follow(self.block.reshape((-1,) + shape[1:]))
            self.block = None
            if following is not None:
                self.start(following)


class ReturnRows:
    def __init__(self, own, borrowed, shards):
        self.own, self.borrowed, self.shards = own, borrowed.astype(jnp.bfloat16), shards
        self.total = None

    def pending(self):
        return self.total is None

    def load(self):
        return (self.borrowed,)

    def fly(self, loads):
        one_sided, turns, sent = row_plan(self.own.shape[1], self.shards)
        if one_sided:
            return (lax.ppermute(loads[0], "rows", [(0, 1), (1, 0)]),)
        gots = []
        for piece, turn in enumerate([-t for t in range(turns, 0, -1)] + list(range(1, turns + 1))):
            block = loads[0][:, piece * sent : (piece + 1) * sent]
            gots.append(lax.ppermute(block, "rows", route(self.shards, turn)))
        return tuple(gots)

    def land(self, loads, gots):
        rows, own = self.own.shape[1], self.own
        one_sided, turns, sent = row_plan(rows, self.shards)
        if one_sided:
            got = gots[0].astype(own.dtype)
            room = [(0, 0)] * own.ndim
            at_end, at_start = list(room), list(room)
            at_end[1], at_start[1] = (rows - sent, 0), (0, rows - sent)
            first = lax.axis_index("rows") == 0
            self.total = own + jnp.where(first, jnp.pad(got, at_end), jnp.pad(got, at_start))
            return
        for piece, got in enumerate(gots):
            span = slice(rows - sent, None) if piece < turns else slice(0, sent)
            own = own.at[:, span].add(got.astype(own.dtype))
        self.total = own


def in_rows(parts):
    flats = [part.reshape(-1) for part in parts]
    return jnp.concatenate([jnp.pad(flat, (0, -flat.size % D)).reshape(-1, D) for flat in flats], axis=0)


def from_rows(rows, parts):
    found, first = [], 0
    for part in parts:
        count = -(-part.size // D)
        found.append(rows[first : first + count].reshape(-1)[: part.size].reshape(part.shape))
        first += count
    return found


def slot(rings, work, *values, wait=()):
    loads = [ring.load() for ring in rings]
    held = lax.optimization_barrier(tuple(values) + sum(loads, ()))
    values, rest = held[: len(values)], held[len(values) :]
    gots = []
    for i, ring in enumerate(rings):
        loads[i], rest = rest[: len(loads[i])], rest[len(loads[i]) :]
        gots.append(ring.fly(loads[i]))
    results = tuple(work(*values))
    held = lax.optimization_barrier(results + tuple(wait) + sum(gots, ()))
    results, rest = held[: len(results)], held[len(results) + len(wait) :]
    for i, ring in enumerate(rings):
        got, rest = rest[: len(gots[i])], rest[len(gots[i]) :]
        ring.land(loads[i], got)
    return results + held[len(results) : len(results) + len(wait)]


def on_device(
    row_shards,
    tokens,
    image_ids,
    timestep,
    norm1_gain,
    norm1_shift,
    time_in_weight,
    time_in_bias,
    time_out_weight,
    time_out_bias,
    mix_weight,
    time_mix_weight,
    position_bias,
    proj_weight,
    proj_bias,
    norm2_gain,
    norm2_shift,
    up_weight,
    up_bias,
    down_weight,
    down_bias,
    cotangent,
):
    seq_rows, local_rows, columns, _ = tokens.shape
    act_tokens = tokens.reshape(seq_rows, local_rows, PACK, GRID, D)
    act_cot = cotangent.reshape(seq_rows, local_rows, PACK, GRID, D)
    token_count = seq_rows * local_rows * columns
    seqs = lax.axis_size("seq")
    place = lax.axis_index("seq")
    images = seqs * seq_rows * PACK
    width_part, freq_part = D // seqs, FREQ // seqs

    def my_part(array, part, axis):
        return lax.dynamic_slice_in_dim(array, place * part, part, axis=axis)

    full_mix = lax.all_gather(mix_weight, "seq", axis=0, tiled=True)
    borrowed, borrowed_at, sent_rows = borrow_rows(act_tokens, row_shards)
    timestep, time_in_weight = lax.optimization_barrier((timestep, time_in_weight, sent_rows))[:2]
    half_width = FREQ // 2
    frequency = jnp.exp(-math.log(10000.0) * jnp.arange(half_width, dtype=jnp.float32) / half_width)

    def time_first(timestep, time_in_weight):
        angles = timestep.astype(jnp.float32).reshape(-1, 1) * frequency
        features = jnp.concatenate([jnp.cos(angles), jnp.sin(angles)], axis=-1).astype(jnp.bfloat16)
        spare = -features.size % D
        features = jnp.pad(features.reshape(-1), (0, spare)).reshape(-1, D)
        both = gather_small(jnp.concatenate([time_in_weight, features], axis=0))
        full_tin = both[:, :freq_part].reshape(FREQ, D)
        features = both[:, freq_part:].reshape(seqs, -1)[:, : seq_rows * PACK * FREQ].reshape(images, FREQ)
        time_pre = jnp.einsum(
            "fd,if->di", my_part(full_tin, width_part, 1), features, preferred_element_type=jnp.float32
        )
        return (features, time_pre + my_part(time_in_bias, width_part, 0)[:, None])

    def time_second(time_pre):
        time_hidden = jax.nn.silu(time_pre).astype(jnp.bfloat16)
        partial = jnp.einsum("fd,fi->di", time_out_weight, time_hidden, preferred_element_type=jnp.float32)
        time_embed = scatter_small(partial.reshape(seqs, width_part, images))
        time_embed = time_embed + my_part(time_out_bias, width_part, 0)[:, None]
        return (time_hidden, time_embed.astype(jnp.bfloat16))

    def time_third(time_embed):
        partial = jnp.einsum("di,de->ie", time_embed, time_mix_weight, preferred_element_type=jnp.float32)
        return (scatter_small(partial.reshape(seqs, seq_rows * PACK, 3 * D), jnp.bfloat16),)

    proj_ring = RingGather(proj_weight)
    features, time_pre = slot([proj_ring], time_first, timestep, time_in_weight)
    time_hidden, time_embed = slot([proj_ring], time_second, time_pre)
    key_at = jnp.concatenate([jnp.arange(local_rows), borrowed_at])
    key_row = lax.axis_index("rows") * local_rows + key_at
    key_rows = jnp.where((key_row >= 0) & (key_row < GRID), key_at, 4 * GRID).astype(jnp.int32)
    table = bias_table(position_bias, key_rows, local_rows)
    time_embed = after(time_embed, table)
    (time_proj,) = slot([proj_ring], time_third, time_embed)
    time_proj = time_proj.reshape(seq_rows, PACK, 3 * D)
    my_features = my_part(features, freq_part, 1)
    block_slots = image_ids[:, ::GRID]
    slot_hot = (block_slots[:, :, None] == jnp.arange(PACK, dtype=jnp.int32)[None, None, :]).astype(
        jnp.float32
    )
    unit_time = jnp.einsum("skp,spe->ske", slot_hot, time_proj, precision=highest)
    ext_tokens = jnp.concatenate([act_tokens, borrowed], axis=1)
    ext_rows = ext_tokens.shape[1]
    ext_count = seq_rows * ext_rows * columns

    normed1, _, inverse_one = norm_forward(ext_tokens.astype(jnp.float32), norm1_gain, norm1_shift)
    normed1 = normed1.astype(jnp.bfloat16)
    mean_one = jnp.mean(act_tokens.astype(jnp.float32), axis=-1, keepdims=True)
    inverse_one = inverse_one[:, :local_rows]
    full_up = lax.all_gather(up_weight, "seq", axis=0, tiled=True)
    down_ring = RingGather(after(down_weight, full_mix[:8, :128]))

    def to_mixed(normed1):
        return ((low_dot(normed1, full_mix) + unit_time[:, None, :, None, :]).astype(jnp.bfloat16),)

    (mixed,) = slot([proj_ring], to_mixed, normed1)
    (attended,) = slot([down_ring, proj_ring], lambda mixed: (attend(mixed, table, local_rows),), mixed)
    full_proj = proj_ring.whole()
    flat_tokens = act_tokens.astype(jnp.float32)

    def second_norm(attended):
        residual = flat_tokens + low_dot(attended, full_proj) + proj_bias
        normed2, unit_two, inverse_two = norm_forward(residual, norm2_gain, norm2_shift)
        return (residual, normed2.astype(jnp.bfloat16), unit_two, inverse_two)

    down_ring.place_pieces()
    attended = after(attended, down_ring.full)
    residual, normed2, unit_two, inverse_two = slot([down_ring], second_norm, attended)

    def to_hidden(normed2):
        pre = low_dot(normed2, full_up) + up_bias
        slope = math.sqrt(2.0 / math.pi)
        square = pre * pre
        bend = jnp.tanh(slope * pre * (1.0 + 0.044715 * square))
        half = 0.5 * (1.0 + bend)
        gelu_slope = half + 0.5 * pre * (1.0 - bend * bend) * (slope * (1.0 + 3.0 * 0.044715 * square))
        return ((pre * half).astype(jnp.bfloat16), gelu_slope.astype(jnp.bfloat16))

    hidden, gelu_slope = slot([down_ring], to_hidden, normed2)
    flat_hidden = hidden.reshape(token_count, FF)
    flat_cot = act_cot.reshape(token_count, D)

    raw = {}

    def weight_down(flat_hidden):
        grad = jnp.einsum("nf,nd->fd", flat_hidden, flat_cot, preferred_element_type=jnp.float32)
        raw["down"] = grad.astype(jnp.bfloat16)
        return (raw["down"],)

    (grad_down_w,) = slot([down_ring], weight_down, flat_hidden)
    full_down = down_ring.whole()
    grad_down_b = jnp.sum(flat_cot, axis=0, dtype=jnp.float32)
    down_part = lax.psum_scatter(raw["down"], "seq", scatter_dimension=0, tiled=True)
    grad_hidden = jnp.einsum(
        "nd,fd->nf", flat_cot, full_down, preferred_element_type=jnp.float32
    )
    grad_pre = (grad_hidden * gelu_slope.reshape(token_count, FF).astype(jnp.float32)).astype(jnp.bfloat16)
    flat_normed2 = normed2.reshape(token_count, D)
    grad_up_w = jnp.einsum("nd,nf->df", flat_normed2, grad_pre, preferred_element_type=jnp.float32)
    grad_up_b = jnp.sum(grad_pre, axis=0, dtype=jnp.float32)
    def back_up(grad_pre):
        grad_normed2 = jnp.einsum("nf,df->nd", grad_pre, full_up, preferred_element_type=jnp.float32)
        return (grad_normed2.reshape(act_tokens.shape),)

    def back_norm(grad_normed2):
        grad_norm_two, grad_gain_two, grad_shift_two = norm_backward(
            grad_normed2, unit_two, inverse_two, norm2_gain
        )
        grad_residual = act_cot.astype(jnp.float32) + grad_norm_two
        grad_branch = grad_residual.astype(jnp.bfloat16).reshape(token_count, D)
        grad_proj_w = jnp.einsum(
            "nd,ne->de", attended.reshape(token_count, D), grad_branch, preferred_element_type=jnp.float32
        ).astype(jnp.bfloat16)
        raw["proj"] = grad_proj_w
        grad_proj_b = jnp.sum(grad_branch, axis=0, dtype=jnp.float32)
        grad_attended = jnp.einsum(
            "ne,de->nd", grad_branch, full_proj, preferred_element_type=jnp.float32
        ).astype(jnp.bfloat16)
        grad_attended = grad_attended.reshape(act_tokens.shape)
        return (grad_residual, grad_gain_two, grad_shift_two, grad_proj_w, grad_proj_b, grad_attended)

    grad_up_w = grad_up_w.astype(jnp.bfloat16)
    (grad_normed2,) = back_up(grad_pre)
    up_sum = RingScatter(grad_up_w)
    (grad_residual, grad_gain_two, grad_shift_two, grad_proj_w, grad_proj_b, grad_attended) = slot(
        [up_sum], back_norm, grad_normed2
    )
    proj_part = lax.psum_scatter(raw["proj"], "seq", scatter_dimension=0, tiled=True)
    part = -(-seq_rows // 2)
    spans = [slice(0, part), slice(part, seq_rows)][: min(2, seq_rows)]
    grad_mixed, grad_tables, grad_units = None, [], []
    for span in spans:
        held = (grad_attended,) if grad_mixed is None else (grad_attended, grad_mixed)
        grad_mixed, grad_table, grad_unit = slot(
            [up_sum], lambda grad, kept=None: attend_back(mixed, grad, table, kept, span, local_rows), *held
        )
        grad_tables.append(grad_table)
        grad_units.append(grad_unit)
    grad_unit = jnp.concatenate(grad_units, axis=0)
    unit_sum, down_sum = RowSum(grad_unit), RowSum(down_part)

    def weight_mix(grad_mixed):
        grad_mix_w = jnp.einsum(
            "nd,ne->de",
            normed1.reshape(ext_count, D),
            grad_mixed.reshape(ext_count, 3 * D),
            preferred_element_type=jnp.float32,
        )
        raw["mix"] = grad_mix_w.astype(jnp.bfloat16)
        return (raw["mix"],)

    (grad_mix_w,) = slot([unit_sum, up_sum, down_sum], weight_mix, grad_mixed)
    found = {}

    def from_time_proj(gathered):
        found["tmix"] = low_dot(time_embed, gathered)
        grad_embed = jnp.einsum("de,ie->di", time_mix_weight, gathered, preferred_element_type=jnp.float32)
        chain.follow = from_embed
        return grad_embed.astype(jnp.bfloat16)

    def from_embed(gathered):
        found["tout"] = jnp.einsum("fi,di->fd", time_hidden, gathered, preferred_element_type=jnp.float32)
        found["tout_b"] = jnp.sum(gathered, axis=1, dtype=jnp.float32)
        silu_back = jax.vjp(jax.nn.silu, time_pre)[1]
        chain.follow = from_pre
        return silu_back(low_dot(time_out_weight, gathered))[0].astype(jnp.bfloat16)

    def from_pre(gathered):
        found["tin"] = jnp.einsum("if,di->fd", my_features, gathered, preferred_element_type=jnp.float32)
        found["tin_b"] = jnp.sum(gathered, axis=1, dtype=jnp.float32)

    grad_time_proj = jnp.einsum("skp,ske->spe", slot_hot, unit_sum.total, precision=highest)
    chain = Chain(grad_time_proj.astype(jnp.bfloat16).reshape(-1, 3 * D), from_time_proj)
    mix_part = lax.psum_scatter(raw["mix"], "seq", scatter_dimension=0, tiled=True)
    first_sums = (grad_proj_b, grad_gain_two, grad_shift_two, grad_up_b, grad_down_b)
    rings = [up_sum, chain]

    def run(work, *values):
        return slot([ring for ring in rings if ring.pending()], work, *values)

    def back_mixed(grad_mixed, span):
        rows = grad_mixed[span]
        grad_in = jnp.einsum("spcge,de->spcgd", rows, full_mix, preferred_element_type=jnp.float32)
        return (grad_in[:, :local_rows], grad_in[:, local_rows:].astype(jnp.bfloat16))

    def back_first(grad_normed1, tokens, grad_residual, span):
        unit_one = (tokens[span].astype(jnp.float32) - mean_one[span]) * inverse_one[span]
        grad_norm_one, gain, shift = norm_backward(grad_normed1, unit_one, inverse_one[span], norm1_gain)
        return ((grad_residual[span] + grad_norm_one).astype(jnp.bfloat16), gain, shift)

    def last_part(hidden, residual, span):
        return ((residual[span] + low_dot(hidden[span], full_down) + down_bias).astype(jnp.bfloat16),)

    (bias_grad,) = run(lambda *pairs: (bias_sum(pairs, key_rows, local_rows),), *grad_tables)
    returned = []
    for span in spans:
        returned.append(ReturnRows(*run(functools.partial(back_mixed, span=span), grad_mixed), row_shards))
        rings.append(returned[-1])
    outputs, tokens_grads, firsts = [], [], []

    def finish(span):
        outputs.extend(run(functools.partial(last_part, span=span), hidden, residual))

    finish(spans[0])
    for span, back in zip(spans, returned):
        firsts.append(run(functools.partial(back_first, span=span), back.total, act_tokens, grad_residual))
        tokens_grads.append(firsts[-1][0])
    grad_gain_one, grad_shift_one = (sum(part) for part in zip(*[first[1:] for first in firsts]))
    late_sums = (grad_gain_one, grad_shift_one, bias_grad) + first_sums
    late_sum = AllSum(in_rows(late_sums))
    proj_sum = RowSum(proj_part)
    rings += [late_sum, proj_sum]
    for span in spans[1:]:
        finish(span)
    output = jnp.concatenate(outputs, axis=0)
    tokens_grad = jnp.concatenate(tokens_grads, axis=0)
    run(lambda: ())
    mix_sum = RowSum(after(mix_part, chain.block))
    mix_got = mix_sum.fly(mix_sum.load())
    while any(ring.pending() for ring in rings):
        run(lambda: ())
    mix_sum.land(mix_sum.load(), mix_got)

    (gain_one, shift_one, bias_total, proj_total, gain_two, shift_two, up_total, down_total) = from_rows(
        late_sum.block, late_sums
    )
    sum_down, sum_up, sum_mix, sum_proj = down_sum.total, up_sum.total, mix_sum.total, proj_sum.total
    sum_tmix, sum_tout, sum_tin = found["tmix"], found["tout"], found["tin"]
    tout_bias, tin_bias = found["tout_b"], found["tin_b"]
    output = output.reshape(tokens.shape)
    tokens_grad = tokens_grad.reshape(tokens.shape)
    return (
        output,
        tokens_grad,
        gain_one,
        shift_one,
        sum_tin,
        tin_bias,
        sum_tout,
        tout_bias,
        sum_mix,
        sum_tmix,
        bias_total,
        sum_proj,
        proj_total,
        gain_two,
        shift_two,
        sum_up,
        up_total,
        sum_down,
        down_total,
    )


def solution(mesh):
    whole, sharded = (P(), P("seq", None))
    acts = P("seq", "rows", None, None)
    return jax.shard_map(
        functools.partial(on_device, mesh.shape["rows"]),
        mesh=mesh,
        in_specs=(
            acts,
            sharded,
            sharded,
            whole,
            whole,
            sharded,
            whole,
            sharded,
            whole,
            sharded,
            sharded,
            whole,
            sharded,
            whole,
            whole,
            whole,
            sharded,
            whole,
            sharded,
            whole,
            acts,
        ),
        out_specs=(
            acts,
            acts,
            whole,
            whole,
            sharded,
            whole,
            sharded,
            whole,
            sharded,
            sharded,
            whole,
            sharded,
            whole,
            whole,
            whole,
            sharded,
            whole,
            sharded,
            whole,
        ),
        check_vma=False,
    )
```
